32 devices in a mesh: grid: 16 (over z, y, x), band: 2 (over core).
Axes of the slice: x: 2, y: 2, z: 4, core: 2. Of those that a mesh axis runs over, the one named last changes fastest.
Arguments:
- orbitals: float32 [16, 16, 32, 32, 128], P('grid', 'band'), may hold values from -24 to 24, as said below
- potential: float32 [16, 32, 32, 128], P('grid'), may hold values from -1 to 1
Outputs:
- rotated: float32 [16, 16, 32, 32, 128], P('grid', 'band')
The draws below stay inside these ranges and needn't reach their ends.
Inputs may be any that keep to these rules, and one draw needn't show every extreme that they name: `orbitals`: real-valued orbital samples.
All inputs are finite; a program needn't handle non-finite values.
Results may differ from the reference program's by a relative error of at most 0.00013.
Values sent between devices are 32-bit elements; how exact they have to be, the bound alone decides.
A program may use at most 128 MiB of HBM per device.

```python
import jax
import jax.numpy as jnp
from jax import lax

ORB = 16
RADIUS = 3
CX = 32
CY = 32
CZ = 128
PX = 2
PY = 2
PZ = 4
NX = 64
NY = 64
NZ = 512
NCELLS = 2097152
N_GRID = 16


def draw_orbitals(key, part):
    shape = (N_GRID, ORB, CX, CY, CZ)
    base = jnp.clip(jax.random.normal(key, shape, jnp.float32), -4.0, 4.0)
    mixed = base + 0.5 * jnp.roll(base, 1, axis=1) + 0.25 * jnp.roll(base, 3, axis=1)
    ramp = 1.0 + 2.0 * jnp.arange(N_GRID, dtype=jnp.float32) / max(N_GRID - 1, 1)
    result = mixed * ramp[:, None, None, None, None]
    return result


def level_of(key, shape, pieces, smallest, largest):
    loudness, own = 1.0, jax.random.fold_in(key, 6)
    for dim, parts in pieces:
        heights = jnp.exp(jax.random.uniform(jax.random.fold_in(own, dim), (parts,), jnp.float32, smallest / len(pieces), largest / len(pieces)))
        loudness = loudness * jnp.repeat(heights, shape[dim] // parts).reshape([-1 if axis == dim else 1 for axis in range(len(shape))])
    return loudness


def setup_inputs(seed: int = 0) -> dict:
    splits = jax.random.split(jax.random.key(seed), 3)
    orbitals = draw_orbitals(jax.random.fold_in(splits[2], 71), 0)
    potential = jnp.clip(jax.random.uniform(splits[1], (N_GRID, CX, CY, CZ), jnp.float32, -1.0, 1.0) * level_of(splits[1], (N_GRID, CX, CY, CZ), ((0, 16),), -0.4, 0.0), -1.0, 1.0)
    return {"orbitals": orbitals, "potential": potential}


COEFFS = (-49.0 / 18.0, 1.5, -0.15, 1.0 / 90.0)
CENTER = 5.75
HALF_WIDTH = 4.75

def apply_hamil(values_in, potential_grid):
    padded = jnp.pad(values_in, RADIUS)
    extent = values_in.shape
    summed = 3.0 * COEFFS[0] * values_in
    for dim_index in range(3):
        for reach in range(1, RADIUS + 1):
            upper_start = [RADIUS, RADIUS, RADIUS]
            lower_start = [RADIUS, RADIUS, RADIUS]
            upper_start[dim_index] = RADIUS + reach
            lower_start[dim_index] = RADIUS - reach
            upper_part = lax.dynamic_slice(padded, upper_start, extent)
            lower_part = lax.dynamic_slice(padded, lower_start, extent)
            summed = summed + COEFFS[reach] * (upper_part + lower_part)
    return -0.5 * summed + potential_grid * values_in

def filter_one(values_in, potential_grid):
    first_term = (apply_hamil(values_in, potential_grid) - CENTER * values_in) / HALF_WIDTH
    return 2.0 * (apply_hamil(first_term, potential_grid) - CENTER * first_term) / HALF_WIDTH - values_in

def reference(orbitals, potential):
    grid_orb = orbitals.reshape(PX, PY, PZ, ORB, CX, CY, CZ).transpose(3, 0, 4, 1, 5, 2, 6).reshape(ORB, NX, NY, NZ)
    grid_pot = potential.reshape(PX, PY, PZ, CX, CY, CZ).transpose(0, 3, 1, 4, 2, 5).reshape(NX, NY, NZ)
    filtered = lax.map(lambda single: filter_one(single, grid_pot), grid_orb)
    flat = filtered.reshape(ORB, NCELLS)
    gram = jnp.einsum('ic,jc->ij', flat, flat, precision=lax.Precision.HIGHEST) / NCELLS
    factor = jnp.linalg.cholesky(gram)
    weights = jax.scipy.linalg.solve_triangular(factor, jnp.eye(ORB, dtype=jnp.float32), lower=True)
    rotated = jnp.dot(weights.astype(jnp.float32), flat.astype(jnp.float32), precision=lax.Precision.HIGHEST, preferred_element_type=jnp.float32)
    rotated = rotated.reshape(ORB, PX, CX, PY, CY, PZ, CZ).transpose(1, 3, 5, 0, 2, 4, 6)
    return rotated.reshape(N_GRID, ORB, CX, CY, CZ)
```

```python
import functools

import jax
import jax.numpy as jnp
from jax import lax
from jax.experimental import pallas as pl
from jax.experimental.pallas import tpu as pltpu
from jax.sharding import PartitionSpec as P

COEFFS = (-49.0 / 18.0, 1.5, -0.15, 1.0 / 90.0)
CENTER = 5.75
HALF_WIDTH = 4.75
TAPS = tuple(-0.5 * c / HALF_WIDTH for c in COEFFS)
DIAGONAL = 3.0 * -0.5 * COEFFS[0] - CENTER
REACH = 3
LEAD = 8
UNROLL = 4
SLOT = 8
F32, BF16 = jnp.float32, jnp.bfloat16
HIGHEST = lax.Precision.HIGHEST
MESH = pl.DeviceIdType.MESH


def layout(devices_grid):
    parts_x = max(2, devices_grid // 32)
    return (parts_x, parts_x, devices_grid // (parts_x * parts_x))


def dot(a, b, contract=((1,), (0,)), precision=None):
    return lax.dot_general(a, b, (contract, ((), ())), precision=precision, preferred_element_type=F32)


def split(value):
    high = value.astype(BF16)
    return high, (value - high.astype(F32)).astype(BF16)


def iota(shape, dim):
    return lax.broadcasted_iota(jnp.int32, shape, dim)


def kernel(parts, volume, x_hbm, v_hbm, pieces, mix, xp, yp, y2, rem, pot, ypack, yrecv, zpack, zrecv, zcorr,
           acc, sums, band_z,
           load_sem, send_sem, recv_sem, y2_send, y2_recv, ar_send, ar_recv):
    count, cx, cy, cz = y2.shape
    nx, ny, nz = parts
    sizes = (nx, ny, nz)
    devices_grid = nx * ny * nz
    strides = (ny * nz, nz, 1)
    grid_index = lax.axis_index("grid")
    band = lax.axis_index("band")
    pos = (grid_index // (ny * nz), grid_index // nz % ny, grid_index % nz)
    tiles = cy // 8
    orbs = 2 * count
    per_pack = cz // SLOT

    def loads(o):
        return pltpu.make_async_copy(
            x_hbm.at[0, o], xp.at[o, REACH:REACH + cx, LEAD:LEAD + cy], load_sem.at[o])

    pot_load = pltpu.make_async_copy(v_hbm.at[0], pot, load_sem.at[count])
    pot_load.start()

    @pl.loop(0, count)
    def _(o):
        loads(o).start()

    barrier = pltpu.get_barrier_semaphore()

    def grid_peer(k):
        return lax.rem(grid_index + k, devices_grid)

    @pl.loop(1, devices_grid)
    def _(k):
        pl.semaphore_signal(barrier, inc=1, device_id={"grid": grid_peer(k)}, device_id_type=MESH)

    pl.semaphore_signal(barrier, inc=1, device_id={"band": 1 - band}, device_id_type=MESH)
    pl.semaphore_wait(barrier, devices_grid)

    can_send = []
    for dim in range(3):
        can_send += [pos[dim] < sizes[dim] - 1, pos[dim] > 0]
    can_recv = [can_send[1], can_send[0], can_send[3], can_send[2], can_send[5], can_send[4]]

    def face(stage, o, d):
        field = (xp, yp)[stage]
        if d == 0:
            src, dst = field.at[o, cx:cx + REACH, LEAD:LEAD + cy], field.at[o, 0:REACH, LEAD:LEAD + cy]
        elif d == 1:
            src = field.at[o, REACH:2 * REACH, LEAD:LEAD + cy]
            dst = field.at[o, cx + REACH:cx + 2 * REACH, LEAD:LEAD + cy]
        elif d < 4:
            src, dst = ypack.at[stage, o, d - 2], yrecv.at[stage, o, d - 2]
        else:
            src, dst = zpack.at[stage, o], zrecv.at[stage, o, d - 4]
        step = strides[d // 2] * (1 - 2 * (d % 2))
        return pltpu.make_async_remote_copy(
            src_ref=src, dst_ref=dst, send_sem=send_sem.at[stage, o, d], recv_sem=recv_sem.at[stage, o, d],
            device_id={"grid": grid_index + step}, device_id_type=MESH)

    for d in range(6):
        @pl.when(jnp.logical_not(can_recv[d]))
        def _(d=d):
            @pl.loop(0, 2 * count)
            def _(i):
                stage, o = i // count, i % count
                if d < 2:
                    start = (0, cx + REACH)[d]
                    for k in range(REACH):
                        zero = jnp.zeros((cy, cz), F32)

                        @pl.when(stage == 0)
                        def _():
                            xp[o, start + k, LEAD:LEAD + cy, :] = zero

                        @pl.when(stage == 1)
                        def _():
                            yp[o, start + k, LEAD:LEAD + cy, :] = zero
                elif d < 4:
                    yrecv[stage, o, d - 2] = jnp.zeros(yrecv.shape[3:], F32)
                else:
                    zrecv[stage, o, d - 4] = jnp.zeros(zrecv.shape[3:], F32)

    def pack_y(stage, field, o):
        for x in range(cx):
            ypack[stage, o, 0, REACH * x:REACH * (x + 1), :] = field[o, REACH + x, LEAD + cy - REACH:LEAD + cy, :]
            ypack[stage, o, 1, REACH * x:REACH * (x + 1), :] = field[o, REACH + x, LEAD:LEAD + REACH, :]

    def unpack_y(stage, field, o):
        for x in range(cx):
            field[o, REACH + x, LEAD - REACH:LEAD, :] = yrecv[stage, o, 0, REACH * x:REACH * (x + 1), :]
            field[o, REACH + x, LEAD + cy:LEAD + cy + REACH, :] = yrecv[stage, o, 1, REACH * x:REACH * (x + 1), :]

    lane = iota((8, cz), 1)
    lane_slot = lane // SLOT

    def pack_z_tile(stage, o, x0, y0, values):
        group, slot = x0 // per_pack, x0 % per_pack
        packed = zpack[stage, o, group, pl.ds(y0, 8), :]
        for u, value in enumerate(values):
            turned = pltpu.roll(value, (slot + u) * SLOT + REACH, 1)
            packed = jnp.where(lane_slot == slot + u, turned, packed)
        zpack[stage, o, group, pl.ds(y0, 8), :] = packed

    def correct_z(stage, o):
        own = zpack[stage, o]
        lanes = iota(own.shape, 2) % SLOT
        from_left = jnp.where(lanes < REACH, zrecv[stage, o, 0] - own, 0.0).reshape(-1, cz)
        right = (lanes >= REACH) & (lanes < 2 * REACH)
        from_right = jnp.where(right, zrecv[stage, o, 1] - own, 0.0).reshape(-1, cz)
        low_side, high_side = 0.0, 0.0
        for r in range(1, REACH + 1):
            low_side = low_side + TAPS[r] * pltpu.roll(from_left, r, 1)
            high_side = high_side + TAPS[r] * pltpu.roll(from_right, cz - r, 1)
        low_side, high_side = low_side.reshape(own.shape), high_side.reshape(own.shape)
        zcorr[...] = jnp.where(lanes < REACH, high_side, jnp.where(right, low_side, 0.0))

    edge = (lane < REACH) | (lane >= cz - REACH)

    def along_z(field, o, x0):
        start = field[o, pl.ds(x0 + REACH, UNROLL), LEAD:LEAD + cy, :].reshape(UNROLL * cy, cz)
        both = dot(jnp.concatenate(split(start), axis=1), band_z[...])
        return both[:, :cz] + both[:, cz:]

    def stencil_tile(field, o, x0, t, turned):
        y0 = 8 * t
        window = [field[o, x0 + i, LEAD + y0:LEAD + y0 + 8, :] for i in range(UNROLL + 2 * REACH)]
        results = []
        group, slot = x0 // per_pack, x0 % per_pack
        corr = zcorr[group, y0:y0 + 8, :]
        for u in range(UNROLL):
            center = window[u + REACH]
            total = pot[x0 + u, y0:y0 + 8, :] * center + turned[u * cy + y0:u * cy + y0 + 8]
            for r in range(1, REACH + 1):
                pair = window[u + REACH + r] + window[u + REACH - r]
                up = field[o, x0 + u + REACH, LEAD + y0 + r:LEAD + y0 + r + 8, :]
                down = field[o, x0 + u + REACH, LEAD + y0 - r:LEAD + y0 - r + 8, :]
                total = total + TAPS[r] * (pair + (up + down))
            fix = pltpu.roll(corr, cz - (slot + u) * SLOT - REACH, 1)
            results.append(total + jnp.where(edge, fix, 0.0))
        return results

    def start_faces(stage, o, sides=tuple(range(6))):
        for d in sides:
            @pl.when(can_send[d])
            def _(d=d):
                face(stage, o, d).start()

    def wait_faces(stage, o):
        for d in range(6):
            @pl.when(can_recv[d])
            def _(d=d):
                face(stage, o, d).wait_recv()

    @pl.loop(0, count)
    def _(o):
        loads(o).wait()
        start_faces(0, o, (0, 1))
        pack_y(0, xp, o)
        start_faces(0, o, (2, 3))

        @pl.loop(0, cx // UNROLL)
        def _(g):
            x0 = g * UNROLL
            for t in range(tiles):
                pack_z_tile(0, o, x0, 8 * t,
                            [xp[o, x0 + u + REACH, LEAD + 8 * t:LEAD + 8 * t + 8, :] for u in range(UNROLL)])

        start_faces(0, o, (4, 5))

    apart = jnp.abs(iota((cz, cz), 0) - iota((cz, cz), 1))
    weights = jnp.zeros((cz, cz), F32)
    for r in range(1, REACH + 1):
        weights = jnp.where((apart == r) | (apart == cz - r), TAPS[r], weights)
    weights_high, weights_low = split(weights)
    band_z[0:cz, 0:cz] = weights_high
    band_z[0:cz, cz:2 * cz] = weights_low
    band_z[cz:2 * cz, 0:cz] = weights_high
    band_z[cz:2 * cz, cz:2 * cz] = jnp.zeros((cz, cz), BF16)
    pot_load.wait()

    @pl.loop(0, cx)
    def _(x):
        pot[x] = (pot[x] + DIAGONAL) * (1.0 / HALF_WIDTH)

    @pl.loop(0, count)
    def _(o):
        wait_faces(0, o)
        unpack_y(0, xp, o)
        correct_z(0, o)

        @pl.loop(0, cx // UNROLL)
        def _(g):
            x0 = g * UNROLL
            turned = along_z(xp, o, x0)
            for t in range(tiles):
                values = stencil_tile(xp, o, x0, t, turned)
                for u in range(UNROLL):
                    yp[o, x0 + u + REACH, LEAD + 8 * t:LEAD + 8 * t + 8, :] = values[u]
                pack_z_tile(1, o, x0, 8 * t, values)

        start_faces(1, o, (0, 1, 4, 5))
        pack_y(1, yp, o)
        start_faces(1, o, (2, 3))

    def halves(value):
        rounded = value.astype(BF16).astype(F32)
        return jnp.concatenate([rounded, value - rounded], axis=0).astype(BF16)

    def hand_over(o):
        return pltpu.make_async_remote_copy(
            src_ref=y2.at[o], dst_ref=rem.at[o], send_sem=y2_send.at[o], recv_sem=y2_recv.at[o],
            device_id={"band": 1 - band}, device_id_type=MESH)

    @pl.loop(0, count)
    def _(o):
        wait_faces(1, o)
        unpack_y(1, yp, o)
        correct_z(1, o)

        @pl.loop(0, cx // UNROLL)
        def _(g):
            x0 = g * UNROLL
            turned = along_z(yp, o, x0)
            for t in range(tiles):
                values = stencil_tile(yp, o, x0, t, turned)
                for u in range(UNROLL):
                    start = xp[o, x0 + u + REACH, LEAD + 8 * t:LEAD + 8 * t + 8, :]
                    value = (values[u] + values[u]) - start
                    y2[o, x0 + u, 8 * t:8 * t + 8, :] = value
                    pieces[x0 + u, t, 0, o] = halves(value)

        hand_over(o).start()

    @pl.loop(0, count)
    def _(o):
        hand_over(o).wait_recv()

        @pl.loop(0, cx // UNROLL)
        def _(g):
            for u in range(UNROLL):
                for t in range(tiles):
                    pieces[g * UNROLL + u, t, 1, o] = halves(rem[o, g * UNROLL + u, 8 * t:8 * t + 8, :])

    side = 16 * orbs
    acc[...] = jnp.zeros_like(acc)

    @pl.loop(0, cx // 2)
    def _(g):
        block = jnp.concatenate(
            [pieces[2 * g + u, t].reshape(side, cz) for u in range(2) for t in range(tiles)], axis=1)
        acc[...] += dot(block, block, ((1,), (1,)))

    same_row = (iota((side, side), 0) % 8) == (iota((side, side), 1) % 8)
    by_orbital = jnp.where(same_row, acc[...], 0.0).reshape(orbs, 16, side).sum(axis=1)
    column = iota((side, cz), 0) // 16
    column = jnp.where(band == 0, column, (column + count) % orbs)
    gathered = dot(by_orbital, (iota((side, cz), 1) == column).astype(F32), precision=HIGHEST)
    total = gathered[:count] + pltpu.roll(gathered[count:], orbs, 1)

    sums[grid_index] = total

    def reduce_copy(k):
        return pltpu.make_async_remote_copy(
            src_ref=sums.at[grid_index], dst_ref=sums.at[grid_index],
            send_sem=ar_send.at[k], recv_sem=ar_recv.at[k],
            device_id={"grid": grid_peer(k)}, device_id_type=MESH)

    @pl.loop(1, devices_grid)
    def _(k):
        reduce_copy(k).start()

    @pl.loop(1, devices_grid)
    def _(k):
        reduce_copy(k).wait_recv()

    total = sums[0]
    for k in range(1, devices_grid):
        total = total + sums[k]

    other = pltpu.roll(total, cz - orbs, 1)
    total = jnp.concatenate([jnp.where(band == 0, total, other), jnp.where(band == 0, other, total)], axis=0)
    row_id, lane_id = iota((orbs, cz), 0), iota((orbs, cz), 1)
    work = jnp.where(lane_id < orbs, total * (1.0 / volume), (lane_id == row_id + orbs).astype(F32))
    for k in range(orbs):
        scale = 1.0 / jnp.sqrt(work[k:k + 1, k:k + 1])
        pivot = work[k:k + 1, :] * scale
        column = jnp.where(row_id > k, work[:, k:k + 1] * scale, 0.0)
        work = jnp.where(row_id == k, pivot, work - column * pivot)

    out_rows = 8 * count
    own_row = iota((out_rows, orbs), 0) // 8 + band * count
    rows_pick = (iota((out_rows, orbs), 1) == own_row).astype(F32)
    lane = iota((cz, side), 1) // 16
    lane = jnp.where(band == 0, lane, (lane + count) % orbs) + orbs
    lanes_pick = (iota((cz, side), 0) == lane).astype(F32)
    full = dot(dot(rows_pick, work, precision=HIGHEST), lanes_pick, precision=HIGHEST)
    full = jnp.where((iota(full.shape, 0) % 8) == (iota(full.shape, 1) % 8), full, 0.0)
    full_high = full.astype(BF16).astype(F32)
    full_low = jnp.where((iota(full.shape, 1) % 16) < 8, full - full_high, 0.0)
    mix[...] = jnp.concatenate([full_high, full_low], axis=0).astype(BF16)

    @pl.loop(0, count)
    def _(o):
        for stage in range(2):
            for d in range(6):
                @pl.when(can_send[d])
                def _(stage=stage, d=d):
                    face(stage, o, d).wait_send()
        hand_over(o).wait_send()

    @pl.loop(1, devices_grid)
    def _(k):
        reduce_copy(k).wait_send()


def rotate(pieces, mix, out_hbm, outv, out_sem):
    cx, tiles, _, count, _, cz = pieces.shape
    rows = 8 * count

    def store(x0):
        return pltpu.make_async_copy(
            outv.at[:, pl.ds(x0, UNROLL)], out_hbm.at[0, :, pl.ds(x0, UNROLL)], out_sem.at[x0 // UNROLL])

    @pl.loop(0, cx // UNROLL)
    def _(g):
        x0 = g * UNROLL
        for u in range(UNROLL):
            for t in range(0, tiles, 2):
                pair = jnp.concatenate(
                    [pieces[x0 + u, t + k].reshape(4 * rows, cz) for k in range(2)], axis=1)
                both = dot(mix[...], pair)
                result = both[:rows] + both[rows:]
                for k in range(2):
                    outv[:, x0 + u, 8 * (t + k):8 * (t + k) + 8, :] = (
                        result[:, k * cz:(k + 1) * cz].reshape(count, 8, cz))
        store(x0).start()

    @pl.loop(0, cx // UNROLL)
    def _(g):
        store(g * UNROLL).wait()


def on_device(orbitals, potential):
    _, count, cx, cy, cz = orbitals.shape
    devices_grid = lax.axis_size("grid")
    parts = layout(devices_grid)
    volume = cx * cy * cz * devices_grid
    orbs = 2 * count
    side = 16 * orbs
    groups = cx * SLOT // cz
    padded = (count, cx + 2 * REACH, cy + 2 * LEAD, cz)
    block = (count, cx, cy, cz)
    dma = pltpu.SemaphoreType.DMA
    any_spec = pl.BlockSpec(memory_space=pl.ANY)
    hbm_spec = pl.BlockSpec(memory_space=pltpu.HBM)
    vmem_spec = pl.BlockSpec(memory_space=pltpu.VMEM)
    pieces, mix = pl.pallas_call(
        functools.partial(kernel, parts, volume),
        out_shape=(pltpu.VMEM((cx, cy // 8, 2, count, 16, cz), BF16), pltpu.VMEM((16 * count, side), BF16)),
        in_specs=[hbm_spec, hbm_spec],
        out_specs=(vmem_spec, vmem_spec),
        scratch_shapes=[
            pltpu.VMEM(padded, F32), pltpu.VMEM(padded, F32),
            pltpu.VMEM(block, F32), pltpu.VMEM(block, F32), pltpu.VMEM((cx, cy, cz), F32),
            pltpu.VMEM((2, count, 2, REACH * cx, cz), F32), pltpu.VMEM((2, count, 2, REACH * cx, cz), F32),
            pltpu.VMEM((2, count, groups, cy, cz), F32), pltpu.VMEM((2, count, 2, groups, cy, cz), F32),
            pltpu.VMEM((groups, cy, cz), F32),
            pltpu.VMEM((side, side), F32),
            pltpu.VMEM((devices_grid, count, cz), F32), pltpu.VMEM((2 * cz, 2 * cz), BF16),
            dma((count + 1,)), dma((2, count, 6)), dma((2, count, 6)), dma((count,)), dma((count,)),
            dma((devices_grid,)), dma((devices_grid,)),
        ],
        compiler_params=pltpu.CompilerParams(
            collective_id=0, has_side_effects=True, vmem_limit_bytes=55 * 1024 * 1024),
    )(orbitals, potential)
    return pl.pallas_call(
        rotate,
        out_shape=jax.ShapeDtypeStruct(orbitals.shape, F32),
        in_specs=[vmem_spec, vmem_spec],
        out_specs=any_spec,
        scratch_shapes=[pltpu.VMEM(block, F32), dma((cx // UNROLL,))],
        compiler_params=pltpu.CompilerParams(vmem_limit_bytes=16 * 1024 * 1024),
    )(pieces, mix)


def solution(mesh):
    in_specs = (P("grid", "band", None, None, None), P("grid", None, None, None))
    out_specs = P("grid", "band", None, None, None)
    return jax.shard_map(
        on_device, mesh=mesh, in_specs=in_specs, out_specs=out_specs, check_vma=False
    )
```

```python
import functools

import jax
import jax.numpy as jnp
from jax import lax
from jax.experimental import pallas as pl
from jax.experimental.pallas import tpu as pltpu
from jax.sharding import PartitionSpec as P

COEFFS = (-49.0 / 18.0, 1.5, -0.15, 1.0 / 90.0)
CENTER = 5.75
HALF_WIDTH = 4.75
TAPS = tuple(-0.5 * c / HALF_WIDTH for c in COEFFS)
DIAGONAL = 3.0 * -0.5 * COEFFS[0] - CENTER
REACH = 3
LEAD = 8
UNROLL = 4
SLOT = 8
F32, BF16 = jnp.float32, jnp.bfloat16
HIGHEST = lax.Precision.HIGHEST
MESH = pl.DeviceIdType.MESH


def layout(devices_grid):
    parts_x = max(2, devices_grid // 32)
    return (parts_x, parts_x, devices_grid // (parts_x * parts_x))


def dot(a, b, contract=((1,), (0,)), precision=None):
    return lax.dot_general(a, b, (contract, ((), ())), precision=precision, preferred_element_type=F32)


def halves(value):
    rounded = value.astype(BF16).astype(F32)
    return jnp.concatenate([rounded, value - rounded], axis=0).astype(BF16)


def iota(shape, dim):
    return lax.broadcasted_iota(jnp.int32, shape, dim)


def kernel(parts, volume, x_hbm, v_hbm, pieces, mix, xp, yp, y2, rem, pot, ypack, yrecv, zpack, zrecv, zcorr,
           acc, sums,
           load_sem, send_sem, recv_sem, y2_send, y2_recv, ar_send, ar_recv):
    count, cx, cy, cz = y2.shape
    nx, ny, nz = parts
    sizes = (nx, ny, nz)
    devices_grid = nx * ny * nz
    strides = (ny * nz, nz, 1)
    grid_index = lax.axis_index("grid")
    band = lax.axis_index("band")
    pos = (grid_index // (ny * nz), grid_index // nz % ny, grid_index % nz)
    tiles = cy // 8
    orbs = 2 * count
    chunks = cx // UNROLL

    def loads(o):
        return pltpu.make_async_copy(
            x_hbm.at[0, o], xp.at[o, REACH:REACH + cx, LEAD:LEAD + cy], load_sem.at[o])

    pot_load = pltpu.make_async_copy(v_hbm.at[0], pot, load_sem.at[count])
    pot_load.start()

    @pl.loop(0, count)
    def _(o):
        loads(o).start()

    barrier = pltpu.get_barrier_semaphore()

    def grid_peer(k):
        return lax.rem(grid_index + k, devices_grid)

    @pl.loop(1, devices_grid)
    def _(k):
        pl.semaphore_signal(barrier, inc=1, device_id={"grid": grid_peer(k)}, device_id_type=MESH)

    pl.semaphore_signal(barrier, inc=1, device_id={"band": 1 - band}, device_id_type=MESH)
    pl.semaphore_wait(barrier, devices_grid)

    can_send = []
    for dim in range(3):
        can_send += [pos[dim] < sizes[dim] - 1, pos[dim] > 0]
    can_recv = [can_send[1], can_send[0], can_send[3], can_send[2], can_send[5], can_send[4]]

    def face(stage, o, d):
        field = (xp, yp)[stage]
        if d == 0:
            src, dst = field.at[o, cx:cx + REACH, LEAD:LEAD + cy], field.at[o, 0:REACH, LEAD:LEAD + cy]
        elif d == 1:
            src = field.at[o, REACH:2 * REACH, LEAD:LEAD + cy]
            dst = field.at[o, cx + REACH:cx + 2 * REACH, LEAD:LEAD + cy]
        elif d < 4:
            src, dst = ypack.at[stage, o, d - 2], yrecv.at[stage, o, d - 2]
        else:
            src, dst = zpack.at[stage, o], zrecv.at[stage, o, d - 4]
        step = strides[d // 2] * (1 - 2 * (d % 2))
        return pltpu.make_async_remote_copy(
            src_ref=src, dst_ref=dst, send_sem=send_sem.at[stage, o, d], recv_sem=recv_sem.at[stage, o, d],
            device_id={"grid": grid_index + step}, device_id_type=MESH)

    for d in range(6):
        @pl.when(jnp.logical_not(can_recv[d]))
        def _(d=d):
            @pl.loop(0, 2 * count)
            def _(i):
                stage, o = i // count, i % count
                if d < 2:
                    start = (0, cx + REACH)[d]
                    for k in range(REACH):
                        zero = jnp.zeros((cy, cz), F32)

                        @pl.when(stage == 0)
                        def _():
                            xp[o, start + k, LEAD:LEAD + cy, :] = zero

                        @pl.when(stage == 1)
                        def _():
                            yp[o, start + k, LEAD:LEAD + cy, :] = zero
                elif d < 4:
                    yrecv[stage, o, d - 2] = jnp.zeros(yrecv.shape[3:], F32)
                else:
                    zrecv[stage, o, d - 4] = jnp.zeros(zrecv.shape[3:], F32)

    def pack_y(stage, field, o):
        for x in range(cx):
            ypack[stage, o, 0, REACH * x:REACH * (x + 1), :] = field[o, REACH + x, LEAD + cy - REACH:LEAD + cy, :]
            ypack[stage, o, 1, REACH * x:REACH * (x + 1), :] = field[o, REACH + x, LEAD:LEAD + REACH, :]

    def unpack_y(stage, field, o):
        for x in range(cx):
            field[o, REACH + x, LEAD - REACH:LEAD, :] = yrecv[stage, o, 0, REACH * x:REACH * (x + 1), :]
            field[o, REACH + x, LEAD + cy:LEAD + cy + REACH, :] = yrecv[stage, o, 1, REACH * x:REACH * (x + 1), :]

    lane = iota((8, cz), 1)
    lane_slot = lane // SLOT

    def pack_z(stage, o, g, values):
        packed = pltpu.roll(values[0], REACH, 1)
        for slot in range(1, len(values)):
            packed = jnp.where(lane_slot == slot, pltpu.roll(values[slot], slot * SLOT + REACH, 1), packed)
        zpack[stage, o, g] = packed

    def correct_z(stage, o):
        own = zpack[stage, o]
        lanes = iota(own.shape, 2) % SLOT
        from_left = jnp.where(lanes < REACH, zrecv[stage, o, 0] - own, 0.0).reshape(-1, cz)
        right = (lanes >= REACH) & (lanes < 2 * REACH)
        from_right = jnp.where(right, zrecv[stage, o, 1] - own, 0.0).reshape(-1, cz)
        low_side, high_side = 0.0, 0.0
        for r in range(1, REACH + 1):
            low_side = low_side + TAPS[r] * pltpu.roll(from_left, r, 1)
            high_side = high_side + TAPS[r] * pltpu.roll(from_right, cz - r, 1)
        low_side, high_side = low_side.reshape(own.shape), high_side.reshape(own.shape)
        zcorr[o] = jnp.where(lanes < REACH, high_side, jnp.where(right, low_side, 0.0))

    edge = (lane < REACH) | (lane >= cz - REACH)

    def stencil(field, o, g, emit):
        x0 = g * UNROLL
        corr = zcorr[o, g]
        for t in range(tiles):
            rows = slice(LEAD + 8 * t, LEAD + 8 * t + 8)
            window = [field[o, x0 + i, rows, :] for i in range(UNROLL + 2 * REACH)]
            for u in range(UNROLL):
                center = window[u + REACH]
                total = pot[x0 + u, 8 * t:8 * t + 8, :] * center
                for r in range(1, REACH + 1):
                    along_x = window[u + REACH + r] + window[u + REACH - r]
                    along_y = (field[o, x0 + u + REACH, rows.start + r:rows.stop + r, :]
                               + field[o, x0 + u + REACH, rows.start - r:rows.stop - r, :])
                    along_z = pltpu.roll(center, r, 1) + pltpu.roll(center, cz - r, 1)
                    total = total + TAPS[r] * ((along_x + along_y) + along_z)
                fix = pltpu.roll(corr, (2 * cz - (t * UNROLL + u) * SLOT - REACH) % cz, 1)
                emit(x0 + u, t, total + jnp.where(edge, fix, 0.0))

    def start_faces(stage, o, sides=tuple(range(6))):
        for d in sides:
            @pl.when(can_send[d])
            def _(d=d):
                face(stage, o, d).start()

    def wait_faces(stage, o, sides=tuple(range(6))):
        for d in sides:
            @pl.when(can_recv[d])
            def _(d=d):
                face(stage, o, d).wait_recv()

    @pl.loop(0, count)
    def _(o):
        loads(o).wait()
        start_faces(0, o, (0, 1))
        pack_y(0, xp, o)
        start_faces(0, o, (2, 3))

        @pl.loop(0, chunks)
        def _(g):
            pack_z(0, o, g, [xp[o, g * UNROLL + u + REACH, LEAD + 8 * t:LEAD + 8 * t + 8, :]
                             for t in range(tiles) for u in range(UNROLL)])

        start_faces(0, o, (4, 5))

    pot_load.wait()

    @pl.loop(0, cx)
    def _(x):
        pot[x] = (pot[x] + DIAGONAL) * (1.0 / HALF_WIDTH)

    @pl.loop(0, count)
    def _(o):
        wait_faces(0, o)
        unpack_y(0, xp, o)
        correct_z(0, o)

        @pl.loop(0, chunks)
        def _(g):
            values = []

            def emit(x, t, value):
                yp[o, x + REACH, LEAD + 8 * t:LEAD + 8 * t + 8, :] = value
                values.append(value)

            stencil(xp, o, g, emit)
            pack_z(1, o, g, values)

        start_faces(1, o, (0, 1, 4, 5))
        pack_y(1, yp, o)
        start_faces(1, o, (2, 3))

    first = jnp.where(can_recv[0], 1, 0)
    last = jnp.where(can_recv[1], chunks - 1, chunks)
    spans = ((0, UNROLL), (UNROLL, cx - 2 * UNROLL), (cx - UNROLL, UNROLL))

    def hand_over(o, part):
        planes = pl.ds(*spans[part])
        return pltpu.make_async_remote_copy(
            src_ref=y2.at[o, planes], dst_ref=rem.at[o, planes], send_sem=y2_send.at[o, part],
            recv_sem=y2_recv.at[o, part], device_id={"band": 1 - band}, device_id_type=MESH)

    def finish(o, g):
        def emit(x, t, value):
            value = (value + value) - xp[o, x + REACH, LEAD + 8 * t:LEAD + 8 * t + 8, :]
            y2[o, x, 8 * t:8 * t + 8, :] = value
            pieces[x, t, 0, o] = halves(value)

        stencil(yp, o, g, emit)

    def take_over(o, g):
        for u in range(UNROLL):
            for t in range(tiles):
                pieces[g * UNROLL + u, t, 1, o] = halves(rem[o, g * UNROLL + u, 8 * t:8 * t + 8, :])

    side = 16 * orbs
    acc[...] = jnp.zeros_like(acc)

    def gram(g):
        block = jnp.concatenate(
            [pieces[g * UNROLL + u, t].reshape(side, cz) for u in range(UNROLL) for t in range(tiles)], axis=1)
        acc[...] += dot(block, block, ((1,), (1,)))

    edges = ((0, 0, can_recv[0]), (2, chunks - 1, can_recv[1]))

    @pl.loop(0, count)
    def _(o):
        wait_faces(1, o, (2, 3, 4, 5))
        unpack_y(1, yp, o)
        correct_z(1, o)

        @pl.loop(first, last)
        def _(g):
            finish(o, g)

        hand_over(o, 1).start()
        for part, _, waits in edges:
            @pl.when(jnp.logical_not(waits))
            def _(part=part):
                hand_over(o, part).start()

    @pl.loop(0, count)
    def _(o):
        hand_over(o, 1).wait_recv()
        for part, _, waits in edges:
            @pl.when(jnp.logical_not(waits))
            def _(part=part):
                hand_over(o, part).wait_recv()

        @pl.loop(first, last)
        def _(g):
            take_over(o, g)

    pl.loop(first, last)(gram)

    @pl.loop(0, count)
    def _(o):
        for part, g, waits in edges:
            @pl.when(waits)
            def _(part=part, g=g):
                wait_faces(1, o, (part // 2,))
                finish(o, g)
                hand_over(o, part).start()

    @pl.loop(0, count)
    def _(o):
        for part, g, waits in edges:
            @pl.when(waits)
            def _(part=part, g=g):
                hand_over(o, part).wait_recv()
                take_over(o, g)

    for part, g, waits in edges:
        @pl.when(waits)
        def _(g=g):
            gram(g)

    same_row = (iota((side, side), 0) % 8) == (iota((side, side), 1) % 8)
    by_orbital = jnp.where(same_row, acc[...], 0.0).reshape(orbs, 16, side).sum(axis=1)
    column = iota((side, cz), 0) // 16
    column = jnp.where(band == 0, column, (column + count) % orbs)
    gathered = dot(by_orbital, (iota((side, cz), 1) == column).astype(F32), precision=HIGHEST)
    total = gathered[:count] + pltpu.roll(gathered[count:], orbs, 1)

    sums[grid_index] = total

    def reduce_copy(k):
        return pltpu.make_async_remote_copy(
            src_ref=sums.at[grid_index], dst_ref=sums.at[grid_index],
            send_sem=ar_send.at[k], recv_sem=ar_recv.at[k],
            device_id={"grid": grid_peer(k)}, device_id_type=MESH)

    @pl.loop(1, devices_grid)
    def _(k):
        reduce_copy(k).start()

    @pl.loop(1, devices_grid)
    def _(k):
        reduce_copy(k).wait_recv()

    total = sums[0]
    for k in range(1, devices_grid):
        total = total + sums[k]

    other = pltpu.roll(total, cz - orbs, 1)
    total = jnp.concatenate([jnp.where(band == 0, total, other), jnp.where(band == 0, other, total)], axis=0)
    row_id, lane_id = iota((orbs, cz), 0), iota((orbs, cz), 1)
    work = jnp.where(lane_id < orbs, total * (1.0 / volume), (lane_id == row_id + orbs).astype(F32))
    for k in range(orbs):
        scale = 1.0 / jnp.sqrt(work[k:k + 1, k:k + 1])
        pivot = work[k:k + 1, :] * scale
        column = jnp.where(row_id > k, work[:, k:k + 1] * scale, 0.0)
        work = jnp.where(row_id == k, pivot, work - column * pivot)

    out_rows = 8 * count
    own_row = iota((out_rows, orbs), 0) // 8 + band * count
    rows_pick = (iota((out_rows, orbs), 1) == own_row).astype(F32)
    lane = iota((cz, side), 1) // 16
    lane = jnp.where(band == 0, lane, (lane + count) % orbs) + orbs
    lanes_pick = (iota((cz, side), 0) == lane).astype(F32)
    full = dot(dot(rows_pick, work, precision=HIGHEST), lanes_pick, precision=HIGHEST)
    full = jnp.where((iota(full.shape, 0) % 8) == (iota(full.shape, 1) % 8), full, 0.0)
    full_high = full.astype(BF16).astype(F32)
    full_low = jnp.where((iota(full.shape, 1) % 16) < 8, full - full_high, 0.0)
    mix[...] = jnp.concatenate([full_high, full_low], axis=0).astype(BF16)

    @pl.loop(0, count)
    def _(o):
        for stage in range(2):
            for d in range(6):
                @pl.when(can_send[d])
                def _(stage=stage, d=d):
                    face(stage, o, d).wait_send()
        for part in range(3):
            hand_over(o, part).wait_send()

    @pl.loop(1, devices_grid)
    def _(k):
        reduce_copy(k).wait_send()


def rotate(pieces, mix, out_hbm, outv, out_sem):
    cx, tiles, _, count, _, cz = pieces.shape
    rows = 8 * count

    def store(x0):
        return pltpu.make_async_copy(
            outv.at[:, pl.ds(x0, UNROLL)], out_hbm.at[0, :, pl.ds(x0, UNROLL)], out_sem.at[x0 // UNROLL])

    @pl.loop(0, cx // UNROLL)
    def _(g):
        x0 = g * UNROLL
        for u in range(UNROLL):
            for t in range(0, tiles, 2):
                pair = jnp.concatenate(
                    [pieces[x0 + u, t + k].reshape(4 * rows, cz) for k in range(2)], axis=1)
                both = dot(mix[...], pair)
                result = both[:rows] + both[rows:]
                for k in range(2):
                    outv[:, x0 + u, 8 * (t + k):8 * (t + k) + 8, :] = (
                        result[:, k * cz:(k + 1) * cz].reshape(count, 8, cz))
        store(x0).start()

    @pl.loop(0, cx // UNROLL)
    def _(g):
        store(g * UNROLL).wait()


def on_device(orbitals, potential):
    _, count, cx, cy, cz = orbitals.shape
    devices_grid = lax.axis_size("grid")
    parts = layout(devices_grid)
    volume = cx * cy * cz * devices_grid
    orbs = 2 * count
    side = 16 * orbs
    chunks = cx // UNROLL
    padded = (count, cx + 2 * REACH, cy + 2 * LEAD, cz)
    block = (count, cx, cy, cz)
    dma = pltpu.SemaphoreType.DMA
    any_spec = pl.BlockSpec(memory_space=pl.ANY)
    hbm_spec = pl.BlockSpec(memory_space=pltpu.HBM)
    vmem_spec = pl.BlockSpec(memory_space=pltpu.VMEM)
    pieces, mix = pl.pallas_call(
        functools.partial(kernel, parts, volume),
        out_shape=(pltpu.VMEM((cx, cy // 8, 2, count, 16, cz), BF16), pltpu.VMEM((16 * count, side), BF16)),
        in_specs=[hbm_spec, hbm_spec],
        out_specs=(vmem_spec, vmem_spec),
        scratch_shapes=[
            pltpu.VMEM(padded, F32), pltpu.VMEM(padded, F32),
            pltpu.VMEM(block, F32), pltpu.VMEM(block, F32), pltpu.VMEM((cx, cy, cz), F32),
            pltpu.VMEM((2, count, 2, REACH * cx, cz), F32), pltpu.VMEM((2, count, 2, REACH * cx, cz), F32),
            pltpu.VMEM((2, count, chunks, 8, cz), F32), pltpu.VMEM((2, count, 2, chunks, 8, cz), F32),
            pltpu.VMEM((count, chunks, 8, cz), F32),
            pltpu.VMEM((side, side), F32),
            pltpu.VMEM((devices_grid, count, cz), F32),
            dma((count + 1,)), dma((2, count, 6)), dma((2, count, 6)), dma((count, 3)), dma((count, 3)),
            dma((devices_grid,)), dma((devices_grid,)),
        ],
        compiler_params=pltpu.CompilerParams(
            collective_id=0, has_side_effects=True, vmem_limit_bytes=55 * 1024 * 1024),
    )(orbitals, potential)
    return pl.pallas_call(
        rotate,
        out_shape=jax.ShapeDtypeStruct(orbitals.shape, F32),
        in_specs=[vmem_spec, vmem_spec],
        out_specs=any_spec,
        scratch_shapes=[pltpu.VMEM(block, F32), dma((cx // UNROLL,))],
        compiler_params=pltpu.CompilerParams(vmem_limit_bytes=16 * 1024 * 1024),
    )(pieces, mix)


def solution(mesh):
    in_specs = (P("grid", "band", None, None, None), P("grid", None, None, None))
    out_specs = P("grid", "band", None, None, None)
    return jax.shard_map(
        on_device, mesh=mesh, in_specs=in_specs, out_specs=out_specs, check_vma=False
    )
```

```python
import functools

import jax
import jax.numpy as jnp
from jax import lax
from jax.experimental import pallas as pl
from jax.experimental.pallas import tpu as pltpu
from jax.sharding import PartitionSpec as P

COEFFS = (-49.0 / 18.0, 1.5, -0.15, 1.0 / 90.0)
CENTER = 5.75
HALF_WIDTH = 4.75
WHOLE = (270.0, -27.0, 2.0)
SCALE = -0.5 / (180.0 * HALF_WIDTH)
DIAGONAL = 3.0 * -0.5 * COEFFS[0] - CENTER
AHEAD = 5
BEHIND = 2
REACH = 3
LEAD = 8
UNROLL = 4
SLOT = 8
F32, BF16 = jnp.float32, jnp.bfloat16
HIGHEST = lax.Precision.HIGHEST
MESH = pl.DeviceIdType.MESH


def layout(devices_grid):
    parts_x = max(2, devices_grid // 32)
    return (parts_x, parts_x, devices_grid // (parts_x * parts_x))


def dot(a, b, contract=((1,), (0,)), precision=None):
    return lax.dot_general(a, b, (contract, ((), ())), precision=precision, preferred_element_type=F32)


def halves(value):
    rounded = value.astype(BF16).astype(F32)
    return jnp.concatenate([rounded, value - rounded], axis=0).astype(BF16)


def iota(shape, dim):
    return lax.broadcasted_iota(jnp.int32, shape, dim)


def kernel(parts, volume, x_hbm, v_hbm, pieces, mix, xp, yp, y2, rem, pot, ypack, yrecv, zpack, zrecv, zcorr,
           acc, sums, band_z, turned,
           load_sem, send_sem, recv_sem, y2_send, y2_recv, ar_send, ar_recv):
    count, cx, cy, cz = y2.shape
    nx, ny, nz = parts
    sizes = (nx, ny, nz)
    devices_grid = nx * ny * nz
    strides = (ny * nz, nz, 1)
    grid_index = lax.axis_index("grid")
    band = lax.axis_index("band")
    pos = (grid_index // (ny * nz), grid_index // nz % ny, grid_index % nz)
    tiles = cy // 8
    orbs = 2 * count
    chunks = cx // UNROLL

    def loads(o):
        return pltpu.make_async_copy(
            x_hbm.at[0, o], xp.at[o, REACH:REACH + cx, LEAD:LEAD + cy], load_sem.at[o])

    pot_load = pltpu.make_async_copy(v_hbm.at[0], pot, load_sem.at[count])
    pot_load.start()

    @pl.loop(0, count)
    def _(o):
        loads(o).start()

    barrier = pltpu.get_barrier_semaphore()

    def grid_peer(k):
        return lax.rem(grid_index + k, devices_grid)

    @pl.loop(1, devices_grid)
    def _(k):
        pl.semaphore_signal(barrier, inc=1, device_id={"grid": grid_peer(k)}, device_id_type=MESH)

    pl.semaphore_signal(barrier, inc=1, device_id={"band": 1 - band}, device_id_type=MESH)
    pl.semaphore_wait(barrier, devices_grid)

    can_send = []
    for dim in range(3):
        can_send += [pos[dim] < sizes[dim] - 1, pos[dim] > 0]
    can_recv = [can_send[1], can_send[0], can_send[3], can_send[2], can_send[5], can_send[4]]

    def face(stage, o, d):
        field = (xp, yp)[stage]
        if d == 0:
            src, dst = field.at[o, cx:cx + REACH, LEAD:LEAD + cy], field.at[o, 0:REACH, LEAD:LEAD + cy]
        elif d == 1:
            src = field.at[o, REACH:2 * REACH, LEAD:LEAD + cy]
            dst = field.at[o, cx + REACH:cx + 2 * REACH, LEAD:LEAD + cy]
        elif d < 4:
            src, dst = ypack.at[stage, o, d - 2], yrecv.at[stage, o, d - 2]
        else:
            src, dst = zpack.at[stage, o], zrecv.at[stage, o, d - 4]
        step = strides[d // 2] * (1 - 2 * (d % 2))
        return pltpu.make_async_remote_copy(
            src_ref=src, dst_ref=dst, send_sem=send_sem.at[stage, o, d], recv_sem=recv_sem.at[stage, o, d],
            device_id={"grid": grid_index + step}, device_id_type=MESH)

    def pack_y(stage, field, o):
        for x in range(cx):
            ypack[stage, o, 0, REACH * x:REACH * (x + 1), :] = field[o, REACH + x, LEAD + cy - REACH:LEAD + cy, :]
            ypack[stage, o, 1, REACH * x:REACH * (x + 1), :] = field[o, REACH + x, LEAD:LEAD + REACH, :]

    def unpack_y(stage, field, o):
        for x in range(cx):
            field[o, REACH + x, LEAD - REACH:LEAD, :] = yrecv[stage, o, 0, REACH * x:REACH * (x + 1), :]
            field[o, REACH + x, LEAD + cy:LEAD + cy + REACH, :] = yrecv[stage, o, 1, REACH * x:REACH * (x + 1), :]

    lane = iota((8, cz), 1)
    lane_slot = lane // SLOT

    def pack_z(stage, o, g, values):
        packed = pltpu.roll(values[0], REACH, 1)
        for slot in range(1, len(values)):
            packed = jnp.where(lane_slot == slot, pltpu.roll(values[slot], slot * SLOT + REACH, 1), packed)
        zpack[stage, o, g] = packed

    def correct_z(stage, o):
        own = zpack[stage, o]
        lanes = iota(own.shape, 2) % SLOT
        from_left = jnp.where(lanes < REACH, zrecv[stage, o, 0] - own, 0.0).reshape(-1, cz)
        right = (lanes >= REACH) & (lanes < 2 * REACH)
        from_right = jnp.where(right, zrecv[stage, o, 1] - own, 0.0).reshape(-1, cz)
        low_side, high_side = 0.0, 0.0
        for r in range(1, REACH + 1):
            low_side = low_side + WHOLE[r - 1] * pltpu.roll(from_left, r, 1)
            high_side = high_side + WHOLE[r - 1] * pltpu.roll(from_right, cz - r, 1)
        low_side, high_side = low_side.reshape(own.shape), high_side.reshape(own.shape)
        zcorr[o] = jnp.where(lanes < REACH, high_side, jnp.where(right, low_side, 0.0))

    edge = (lane < REACH) | (lane >= cz - REACH)

    def turn(field, o, g):
        start = field[o, pl.ds(g * UNROLL + REACH, UNROLL), LEAD:LEAD + cy, :].reshape(UNROLL * cy, cz)
        high = start.astype(BF16)
        low = (start - high.astype(F32)).astype(BF16)
        return dot(jnp.concatenate([high, low], axis=1), band_z[...])

    def stencil(field, o, g, following, emit):
        x0 = g * UNROLL
        coming = turn(field, *following)
        corr = zcorr[o, g]
        for t in range(tiles):
            rows = slice(LEAD + 8 * t, LEAD + 8 * t + 8)
            window = [field[o, x0 + i, rows, :] for i in range(UNROLL + 2 * REACH)]
            for u in range(UNROLL):
                total = pot[x0 + u, 8 * t:8 * t + 8, :] * window[u + REACH] + turned[u * cy + 8 * t:u * cy + 8 * t + 8]
                for r in range(1, REACH + 1):
                    along_x = window[u + REACH + r] + window[u + REACH - r]
                    along_y = (field[o, x0 + u + REACH, rows.start + r:rows.stop + r, :]
                               + field[o, x0 + u + REACH, rows.start - r:rows.stop - r, :])
                    total = total + WHOLE[r - 1] * (along_x + along_y)
                fix = pltpu.roll(corr, (2 * cz - (t * UNROLL + u) * SLOT - REACH) % cz, 1)
                emit(x0 + u, t, total + jnp.where(edge, fix, 0.0))
        turned[...] = coming

    def start_faces(stage, o, sides=tuple(range(6))):
        for d in sides:
            @pl.when(can_send[d])
            def _(d=d):
                face(stage, o, d).start()

    def wait_faces(stage, o, sides=tuple(range(6))):
        for d in sides:
            @pl.when(can_recv[d])
            def _(d=d):
                face(stage, o, d).wait_recv()

    for d in range(6):
        @pl.when(jnp.logical_not(can_recv[d]))
        def _(d=d):
            @pl.loop(0, 2 * count)
            def _(i):
                stage, o = i // count, i % count
                if d < 2:
                    start = (0, cx + REACH)[d]
                    for k in range(REACH):
                        zero = jnp.zeros((cy, cz), F32)

                        @pl.when(stage == 0)
                        def _():
                            xp[o, start + k, LEAD:LEAD + cy, :] = zero

                        @pl.when(stage == 1)
                        def _():
                            yp[o, start + k, LEAD:LEAD + cy, :] = zero
                elif d < 4:
                    yrecv[stage, o, d - 2] = jnp.zeros(yrecv.shape[3:], F32)
                else:
                    zrecv[stage, o, d - 4] = jnp.zeros(zrecv.shape[3:], F32)

    def send_start(o):
        start_faces(0, o, (0, 1))
        pack_y(0, xp, o)
        start_faces(0, o, (2, 3))

        @pl.loop(0, chunks // 4)
        def _(q):
            for k in range(4):
                g = 4 * q + k
                pack_z(0, o, g, [xp[o, g * UNROLL + u + REACH, LEAD + 8 * t:LEAD + 8 * t + 8, :]
                                 for t in range(tiles) for u in range(UNROLL)])

        start_faces(0, o, (4, 5))

    @pl.loop(0, count)
    def _(o):
        loads(o).wait()

        @pl.when(o < AHEAD)
        def _():
            send_start(o)

    apart = jnp.abs(iota((2 * cz, cz), 0) % cz - iota((2 * cz, cz), 1))
    weights = jnp.zeros((2 * cz, cz), F32)
    for r in range(1, REACH + 1):
        weights = jnp.where((apart == r) | (apart == cz - r), WHOLE[r - 1], weights)
    band_z[...] = weights.astype(BF16)
    pot_load.wait()

    @pl.loop(0, cx)
    def _(x):
        pot[x] = (pot[x] + DIAGONAL) * (1.0 / HALF_WIDTH / SCALE)

    def after(o, g, low, high):
        more = g + 1 < high
        return jnp.where(more, o, jnp.minimum(o + 1, count - 1)), jnp.where(more, g + 1, low)

    turned[...] = turn(xp, 0, 0)

    @pl.loop(0, count)
    def _(o):
        wait_faces(0, o)

        @pl.when(o + AHEAD < count)
        def _():
            send_start(o + AHEAD)

        unpack_y(0, xp, o)
        correct_z(0, o)

        @pl.loop(0, chunks)
        def _(g):
            values = []

            def emit(x, t, value):
                yp[o, x + REACH, LEAD + 8 * t:LEAD + 8 * t + 8, :] = value
                values.append(value)

            stencil(xp, o, g, after(o, g, 0, chunks), emit)
            pack_z(1, o, g, values)

        start_faces(1, o, (4, 5))
        pack_y(1, yp, o)
        start_faces(1, o, (2, 3))

        @pl.when(o >= count - BEHIND)
        def _():
            start_faces(1, o - (count - BEHIND), (0, 1))

    first = jnp.where(can_recv[0], 1, 0)
    last = jnp.where(can_recv[1], chunks - 1, chunks)
    spans = ((0, UNROLL), (UNROLL, cx - 2 * UNROLL), (cx - UNROLL, UNROLL))

    def hand_over(o, part):
        planes = pl.ds(*spans[part])
        return pltpu.make_async_remote_copy(
            src_ref=y2.at[o, planes], dst_ref=rem.at[o, planes], send_sem=y2_send.at[o, part],
            recv_sem=y2_recv.at[o, part], device_id={"band": 1 - band}, device_id_type=MESH)

    def finish(o, g, following):
        def emit(x, t, value):
            start = xp[o, x + REACH, LEAD + 8 * t:LEAD + 8 * t + 8, :]
            value = value - start * (0.5 / SCALE / SCALE)
            y2[o, x, 8 * t:8 * t + 8, :] = value
            pieces[x, t, 0, o] = halves(value)

        stencil(yp, o, g, following, emit)

    def take_over(o, g):
        for u in range(UNROLL):
            for t in range(tiles):
                pieces[g * UNROLL + u, t, 1, o] = halves(rem[o, g * UNROLL + u, 8 * t:8 * t + 8, :])

    side = 16 * orbs
    acc[...] = jnp.zeros_like(acc)

    def gram(g):
        block = jnp.concatenate(
            [pieces[g * UNROLL + u, t].reshape(side, cz) for u in range(UNROLL) for t in range(tiles)], axis=1)
        acc[...] += dot(block, block, ((1,), (1,)))

    edges = ((0, 0, can_recv[0]), (2, chunks - 1, can_recv[1]))

    turned[...] = turn(yp, 0, first)

    @pl.loop(0, count)
    def _(o):
        @pl.when(o + BEHIND < count)
        def _():
            start_faces(1, o + BEHIND, (0, 1))

        wait_faces(1, o, (2, 3, 4, 5))
        unpack_y(1, yp, o)
        correct_z(1, o)

        @pl.loop(first, last)
        def _(g):
            finish(o, g, after(o, g, first, last))

        hand_over(o, 1).start()
        for part, _, waits in edges:
            @pl.when(jnp.logical_not(waits))
            def _(part=part):
                hand_over(o, part).start()

    @pl.loop(0, count)
    def _(o):
        hand_over(o, 1).wait_recv()
        for part, _, waits in edges:
            @pl.when(jnp.logical_not(waits))
            def _(part=part):
                hand_over(o, part).wait_recv()

        @pl.loop(first, last)
        def _(g):
            take_over(o, g)

    pl.loop(first, last)(gram)

    for part, g, waits in edges:
        @pl.when(waits)
        def _(part=part, g=g):
            turned[...] = turn(yp, 0, g)

            @pl.loop(0, count)
            def _(o):
                wait_faces(1, o, (part // 2,))
                finish(o, g, (jnp.minimum(o + 1, count - 1), g))
                hand_over(o, part).start()

    @pl.loop(0, count)
    def _(o):
        for part, g, waits in edges:
            @pl.when(waits)
            def _(part=part, g=g):
                hand_over(o, part).wait_recv()
                take_over(o, g)

    for part, g, waits in edges:
        @pl.when(waits)
        def _(g=g):
            gram(g)

    same_row = (iota((side, side), 0) % 8) == (iota((side, side), 1) % 8)
    by_orbital = jnp.where(same_row, acc[...], 0.0).reshape(orbs, 16, side).sum(axis=1)
    column = iota((side, cz), 0) // 16
    column = jnp.where(band == 0, column, (column + count) % orbs)
    gathered = dot(by_orbital, (iota((side, cz), 1) == column).astype(F32), precision=HIGHEST)
    total = gathered[:count] + pltpu.roll(gathered[count:], orbs, 1)

    sums[grid_index] = total

    def reduce_copy(k):
        return pltpu.make_async_remote_copy(
            src_ref=sums.at[grid_index], dst_ref=sums.at[grid_index],
            send_sem=ar_send.at[k], recv_sem=ar_recv.at[k],
            device_id={"grid": grid_peer(k)}, device_id_type=MESH)

    @pl.loop(1, devices_grid)
    def _(k):
        reduce_copy(k).start()

    @pl.loop(1, devices_grid)
    def _(k):
        reduce_copy(k).wait_recv()

    total = sums[0]
    for k in range(1, devices_grid):
        total = total + sums[k]

    other = pltpu.roll(total, cz - orbs, 1)
    total = jnp.concatenate([jnp.where(band == 0, total, other), jnp.where(band == 0, other, total)], axis=0)
    row_id, lane_id = iota((orbs, cz), 0), iota((orbs, cz), 1)
    work = jnp.where(lane_id < orbs, total * (1.0 / volume), (lane_id == row_id + orbs).astype(F32))
    for k in range(orbs):
        scale = 1.0 / jnp.sqrt(work[k:k + 1, k:k + 1])
        pivot = work[k:k + 1, :] * scale
        column = jnp.where(row_id > k, work[:, k:k + 1] * scale, 0.0)
        work = jnp.where(row_id == k, pivot, work - column * pivot)

    out_rows = 8 * count
    own_row = iota((out_rows, orbs), 0) // 8 + band * count
    rows_pick = (iota((out_rows, orbs), 1) == own_row).astype(F32)
    lane = iota((cz, side), 1) // 16
    lane = jnp.where(band == 0, lane, (lane + count) % orbs) + orbs
    lanes_pick = (iota((cz, side), 0) == lane).astype(F32)
    full = dot(dot(rows_pick, work, precision=HIGHEST), lanes_pick, precision=HIGHEST)
    full = jnp.where((iota(full.shape, 0) % 8) == (iota(full.shape, 1) % 8), full, 0.0)
    full_high = full.astype(BF16).astype(F32)
    full_low = jnp.where((iota(full.shape, 1) % 16) < 8, full - full_high, 0.0)
    mix[...] = jnp.concatenate([full_high, full_low], axis=0).astype(BF16)

    @pl.loop(0, count)
    def _(o):
        for stage in range(2):
            for d in range(6):
                @pl.when(can_send[d])
                def _(stage=stage, d=d):
                    face(stage, o, d).wait_send()
        for part in range(3):
            hand_over(o, part).wait_send()

    @pl.loop(1, devices_grid)
    def _(k):
        reduce_copy(k).wait_send()


def rotate(pieces, mix, out_hbm, outv, out_sem):
    cx, tiles, _, count, _, cz = pieces.shape
    rows = 8 * count

    def store(x0):
        return pltpu.make_async_copy(
            outv.at[:, pl.ds(x0, UNROLL)], out_hbm.at[0, :, pl.ds(x0, UNROLL)], out_sem.at[x0 // UNROLL])

    @pl.loop(0, cx // UNROLL)
    def _(g):
        x0 = g * UNROLL
        for u in range(UNROLL):
            for t in range(0, tiles, 2):
                pair = jnp.concatenate(
                    [pieces[x0 + u, t + k].reshape(4 * rows, cz) for k in range(2)], axis=1)
                both = dot(mix[...], pair)
                result = both[:rows] + both[rows:]
                for k in range(2):
                    outv[:, x0 + u, 8 * (t + k):8 * (t + k) + 8, :] = (
                        result[:, k * cz:(k + 1) * cz].reshape(count, 8, cz))
        store(x0).start()

    @pl.loop(0, cx // UNROLL)
    def _(g):
        store(g * UNROLL).wait()


def on_device(orbitals, potential):
    _, count, cx, cy, cz = orbitals.shape
    devices_grid = lax.axis_size("grid")
    parts = layout(devices_grid)
    volume = cx * cy * cz * devices_grid
    orbs = 2 * count
    side = 16 * orbs
    chunks = cx // UNROLL
    padded = (count, cx + 2 * REACH, cy + 2 * LEAD, cz)
    block = (count, cx, cy, cz)
    dma = pltpu.SemaphoreType.DMA
    any_spec = pl.BlockSpec(memory_space=pl.ANY)
    hbm_spec = pl.BlockSpec(memory_space=pltpu.HBM)
    vmem_spec = pl.BlockSpec(memory_space=pltpu.VMEM)
    pieces, mix = pl.pallas_call(
        functools.partial(kernel, parts, volume),
        out_shape=(pltpu.VMEM((cx, cy // 8, 2, count, 16, cz), BF16), pltpu.VMEM((16 * count, side), BF16)),
        in_specs=[hbm_spec, hbm_spec],
        out_specs=(vmem_spec, vmem_spec),
        scratch_shapes=[
            pltpu.VMEM(padded, F32), pltpu.VMEM(padded, F32),
            pltpu.VMEM(block, F32), pltpu.VMEM(block, F32), pltpu.VMEM((cx, cy, cz), F32),
            pltpu.VMEM((2, count, 2, REACH * cx, cz), F32), pltpu.VMEM((2, count, 2, REACH * cx, cz), F32),
            pltpu.VMEM((2, count, chunks, 8, cz), F32), pltpu.VMEM((2, count, 2, chunks, 8, cz), F32),
            pltpu.VMEM((count, chunks, 8, cz), F32),
            pltpu.VMEM((side, side), F32),
            pltpu.VMEM((devices_grid, count, cz), F32), pltpu.VMEM((2 * cz, cz), BF16),
            pltpu.VMEM((UNROLL * cy, cz), F32),
            dma((count + 1,)), dma((2, count, 6)), dma((2, count, 6)), dma((count, 3)), dma((count, 3)),
            dma((devices_grid,)), dma((devices_grid,)),
        ],
        compiler_params=pltpu.CompilerParams(
            collective_id=0, has_side_effects=True, vmem_limit_bytes=55 * 1024 * 1024),
    )(orbitals, potential)
    return pl.pallas_call(
        rotate,
        out_shape=jax.ShapeDtypeStruct(orbitals.shape, F32),
        in_specs=[vmem_spec, vmem_spec],
        out_specs=any_spec,
        scratch_shapes=[pltpu.VMEM(block, F32), dma((cx // UNROLL,))],
        compiler_params=pltpu.CompilerParams(vmem_limit_bytes=16 * 1024 * 1024),
    )(pieces, mix)


def solution(mesh):
    in_specs = (P("grid", "band", None, None, None), P("grid", None, None, None))
    out_specs = P("grid", "band", None, None, None)
    return jax.shard_map(
        on_device, mesh=mesh, in_specs=in_specs, out_specs=out_specs, check_vma=False
    )
```

```python
import functools

import jax
import jax.numpy as jnp
from jax import lax
from jax.experimental import pallas as pl
from jax.experimental.pallas import tpu as pltpu
from jax.sharding import PartitionSpec as P

COEFFS = (-49.0 / 18.0, 1.5, -0.15, 1.0 / 90.0)
CENTER = 5.75
HALF_WIDTH = 4.75
WHOLE = (270.0, -27.0, 2.0)
SCALE = -0.5 / (180.0 * HALF_WIDTH)
DIAGONAL = 3.0 * -0.5 * COEFFS[0] - CENTER
AHEAD = 6
BEHIND = 2
REACH = 3
LEAD = 8
UNROLL = 4
SLOT = 8
F32, BF16 = jnp.float32, jnp.bfloat16
MESH = pl.DeviceIdType.MESH


def layout(devices_grid):
    parts_x = max(2, devices_grid // 32)
    return (parts_x, parts_x, devices_grid // (parts_x * parts_x))


def dot(a, b, contract=((1,), (0,)), precision=None):
    return lax.dot_general(a, b, (contract, ((), ())), precision=precision, preferred_element_type=F32)


def halves(value):
    rounded = value.astype(BF16).astype(F32)
    return jnp.concatenate([rounded, value - rounded], axis=0).astype(BF16)


def iota(shape, dim):
    return lax.broadcasted_iota(jnp.int32, shape, dim)


def kernel(parts, volume, x_hbm, v_hbm, pieces, mix, xp, yp, y2, rem, pot, ypack, yrecv, zpack, zrecv, zcorr,
           acc, acc_far, sums, band_z, turned,
           load_sem, send_sem, recv_sem, y2_send, y2_recv, acc_send, acc_recv, ar_send, ar_recv):
    count, cx, cy, cz = y2.shape
    nx, ny, nz = parts
    sizes = (nx, ny, nz)
    devices_grid = nx * ny * nz
    strides = (ny * nz, nz, 1)
    grid_index = lax.axis_index("grid")
    band = lax.axis_index("band")
    pos = (grid_index // (ny * nz), grid_index // nz % ny, grid_index % nz)
    tiles = cy // 8
    orbs = 2 * count
    chunks = cx // UNROLL

    def loads(o):
        return pltpu.make_async_copy(
            x_hbm.at[0, o], xp.at[o, REACH:REACH + cx, LEAD:LEAD + cy], load_sem.at[o])

    pot_load = pltpu.make_async_copy(v_hbm.at[0], pot, load_sem.at[count])
    pot_load.start()

    @pl.loop(0, count)
    def _(o):
        loads(o).start()

    barrier = pltpu.get_barrier_semaphore()

    def grid_peer(k):
        return lax.rem(grid_index + k, devices_grid)

    @pl.loop(1, devices_grid)
    def _(k):
        pl.semaphore_signal(barrier, inc=1, device_id={"grid": grid_peer(k)}, device_id_type=MESH)

    pl.semaphore_signal(barrier, inc=1, device_id={"band": 1 - band}, device_id_type=MESH)
    pl.semaphore_wait(barrier, devices_grid)

    can_send = []
    for dim in range(3):
        can_send += [pos[dim] < sizes[dim] - 1, pos[dim] > 0]
    can_recv = [can_send[1], can_send[0], can_send[3], can_send[2], can_send[5], can_send[4]]

    def face(stage, o, d):
        field = (xp, yp)[stage]
        if d == 0:
            src, dst = field.at[o, cx:cx + REACH, LEAD:LEAD + cy], field.at[o, 0:REACH, LEAD:LEAD + cy]
        elif d == 1:
            src = field.at[o, REACH:2 * REACH, LEAD:LEAD + cy]
            dst = field.at[o, cx + REACH:cx + 2 * REACH, LEAD:LEAD + cy]
        elif d < 4:
            src, dst = ypack.at[stage, o, d - 2], yrecv.at[stage, o, d - 2]
        else:
            src, dst = zpack.at[stage, o], zrecv.at[stage, o, d - 4]
        if stage == 0 and d < 2:
            src = x_hbm.at[0, o, cx - REACH:cx] if d == 0 else x_hbm.at[0, o, 0:REACH]
        step = strides[d // 2] * (1 - 2 * (d % 2))
        return pltpu.make_async_remote_copy(
            src_ref=src, dst_ref=dst, send_sem=send_sem.at[stage, o, d], recv_sem=recv_sem.at[stage, o, d],
            device_id={"grid": grid_index + step}, device_id_type=MESH)

    def pack_y(stage, field, o):
        for x in range(cx):
            ypack[stage, o, 0, REACH * x:REACH * (x + 1), :] = field[o, REACH + x, LEAD + cy - REACH:LEAD + cy, :]
            ypack[stage, o, 1, REACH * x:REACH * (x + 1), :] = field[o, REACH + x, LEAD:LEAD + REACH, :]

    def unpack_y(stage, field, o):
        for x in range(cx):
            field[o, REACH + x, LEAD - REACH:LEAD, :] = yrecv[stage, o, 0, REACH * x:REACH * (x + 1), :]
            field[o, REACH + x, LEAD + cy:LEAD + cy + REACH, :] = yrecv[stage, o, 1, REACH * x:REACH * (x + 1), :]

    lane = iota((8, cz), 1)
    lane_slot = lane // SLOT

    def pack_z(stage, o, g, values):
        packed = pltpu.roll(values[0], REACH, 1)
        for slot in range(1, len(values)):
            packed = jnp.where(lane_slot == slot, pltpu.roll(values[slot], slot * SLOT + REACH, 1), packed)
        zpack[stage, o, g] = packed

    def correct_z(stage, o):
        own = zpack[stage, o]
        lanes = iota(own.shape, 2) % SLOT
        from_left = jnp.where(lanes < REACH, zrecv[stage, o, 0] - own, 0.0).reshape(-1, cz)
        right = (lanes >= REACH) & (lanes < 2 * REACH)
        from_right = jnp.where(right, zrecv[stage, o, 1] - own, 0.0).reshape(-1, cz)
        low_side, high_side = 0.0, 0.0
        for r in range(1, REACH + 1):
            low_side = low_side + WHOLE[r - 1] * pltpu.roll(from_left, r, 1)
            high_side = high_side + WHOLE[r - 1] * pltpu.roll(from_right, cz - r, 1)
        low_side, high_side = low_side.reshape(own.shape), high_side.reshape(own.shape)
        zcorr[o] = jnp.where(lanes < REACH, high_side, jnp.where(right, low_side, 0.0))

    edge = (lane < REACH) | (lane >= cz - REACH)

    def turn(field, o, some):
        start = jnp.concatenate(
            [field[o, pl.ds(g * UNROLL + REACH, UNROLL), LEAD:LEAD + cy, :].reshape(UNROLL * cy, cz) for g in some])
        high = start.astype(BF16)
        low = (start - high.astype(F32)).astype(BF16)
        return dot(jnp.concatenate([high, low], axis=1), band_z[...])

    def stencil(field, o, some, following, emit):
        coming = turn(field, *following)
        for place, g in enumerate(some):
            x0 = g * UNROLL
            corr = zcorr[o, g]
            for t in range(tiles):
                rows = slice(LEAD + 8 * t, LEAD + 8 * t + 8)
                window = [field[o, x0 + i, rows, :] for i in range(UNROLL + 2 * REACH)]
                for u in range(UNROLL):
                    row = (place * UNROLL + u) * cy + 8 * t
                    total = pot[x0 + u, 8 * t:8 * t + 8, :] * window[u + REACH] + turned[row:row + 8]
                    for r in range(1, REACH + 1):
                        along_x = window[u + REACH + r] + window[u + REACH - r]
                        along_y = (field[o, x0 + u + REACH, rows.start + r:rows.stop + r, :]
                                   + field[o, x0 + u + REACH, rows.start - r:rows.stop - r, :])
                        total = total + WHOLE[r - 1] * (along_x + along_y)
                    fix = pltpu.roll(corr, (2 * cz - (t * UNROLL + u) * SLOT - REACH) % cz, 1)
                    emit(x0 + u, t, total + jnp.where(edge, fix, 0.0))
        turned[0:coming.shape[0]] = coming

    def wait_faces(stage, o, sides=tuple(range(6))):
        for d in sides:
            @pl.when(can_recv[d])
            def _(d=d):
                face(stage, o, d).wait_recv()

    def start_faces(stage, o, sides=tuple(range(6))):
        for d in sides:
            @pl.when(can_send[d])
            def _(d=d):
                face(stage, o, d).start()

    for o in range(AHEAD):
        start_faces(0, o, (0, 1))

    for d in range(6):
        @pl.when(jnp.logical_not(can_recv[d]))
        def _(d=d):
            @pl.loop(0, 2 * count)
            def _(i):
                stage, o = i // count, i % count
                if d < 2:
                    start = (0, cx + REACH)[d]
                    for k in range(REACH):
                        zero = jnp.zeros((cy, cz), F32)

                        @pl.when(stage == 0)
                        def _():
                            xp[o, start + k, LEAD:LEAD + cy, :] = zero

                        @pl.when(stage == 1)
                        def _():
                            yp[o, start + k, LEAD:LEAD + cy, :] = zero
                elif d < 4:
                    yrecv[stage, o, d - 2] = jnp.zeros(yrecv.shape[3:], F32)
                else:
                    zrecv[stage, o, d - 4] = jnp.zeros(zrecv.shape[3:], F32)

    def send_start(o):
        pack_y(0, xp, o)
        start_faces(0, o, (2, 3))

        @pl.loop(0, chunks // 4)
        def _(q):
            for k in range(4):
                g = 4 * q + k
                pack_z(0, o, g, [xp[o, g * UNROLL + u + REACH, LEAD + 8 * t:LEAD + 8 * t + 8, :]
                                 for t in range(tiles) for u in range(UNROLL)])

        start_faces(0, o, (4, 5))

    @pl.loop(0, count)
    def _(o):
        loads(o).wait()

        @pl.when(o < AHEAD)
        def _():
            send_start(o)

    apart = jnp.abs(iota((2 * cz, cz), 0) % cz - iota((2 * cz, cz), 1))
    weights = jnp.zeros((2 * cz, cz), F32)
    for r in range(1, REACH + 1):
        weights = jnp.where((apart == r) | (apart == cz - r), WHOLE[r - 1], weights)
    band_z[...] = weights.astype(BF16)
    pot_load.wait()

    @pl.loop(0, cx)
    def _(x):
        pot[x] = (pot[x] + DIAGONAL) * (1.0 / HALF_WIDTH / SCALE)

    def pair(q, low, high):
        return low + 2 * q, jnp.minimum(low + 2 * q + 1, high - 1)

    def after(o, q, low, high):
        more = 2 * q + 2 < high - low
        return (jnp.where(more, o, jnp.minimum(o + 1, count - 1)), pair(jnp.where(more, q + 1, 0), low, high))

    turned[...] = turn(xp, 0, (0, 1))

    @pl.loop(0, count)
    def _(o):
        wait_faces(0, o)

        @pl.when(o + AHEAD < count)
        def _():
            start_faces(0, o + AHEAD, (0, 1))
            send_start(o + AHEAD)

        unpack_y(0, xp, o)
        correct_z(0, o)

        @pl.loop(0, chunks // 2)
        def _(q):
            values = []

            def emit(x, t, value):
                yp[o, x + REACH, LEAD + 8 * t:LEAD + 8 * t + 8, :] = value
                values.append(value)

            stencil(xp, o, pair(q, 0, chunks), after(o, q, 0, chunks), emit)
            for k in range(2):
                pack_z(1, o, 2 * q + k, values[k * UNROLL * tiles:(k + 1) * UNROLL * tiles])

        start_faces(1, o, (4, 5))
        pack_y(1, yp, o)
        start_faces(1, o, (2, 3))

        @pl.when(o >= count - BEHIND)
        def _():
            start_faces(1, o - (count - BEHIND), (0, 1))

    first = jnp.where(can_recv[0], 1, 0)
    last = jnp.where(can_recv[1], chunks - 1, chunks)
    spans = ((0, UNROLL), (UNROLL, cx - 2 * UNROLL), (cx - UNROLL, UNROLL))

    def hand_over(o, part):
        planes = pl.ds(*spans[part])
        return pltpu.make_async_remote_copy(
            src_ref=y2.at[o, planes], dst_ref=rem.at[o, planes], send_sem=y2_send.at[o, part],
            recv_sem=y2_recv.at[o, part], device_id={"band": 1 - band}, device_id_type=MESH)

    def finish(o, some, following):
        def emit(x, t, value):
            start = xp[o, x + REACH, LEAD + 8 * t:LEAD + 8 * t + 8, :]
            value = value - start * (0.5 / SCALE / SCALE)
            y2[o, x, 8 * t:8 * t + 8, :] = value
            pieces[x, t, band, o] = halves(value)

        stencil(yp, o, some, following, emit)

    def take_over(o, g):
        for u in range(UNROLL):
            for t in range(tiles):
                pieces[g * UNROLL + u, t, 1 - band, o] = halves(rem[o, g * UNROLL + u, 8 * t:8 * t + 8, :])

    side = 16 * orbs
    acc[...] = jnp.zeros_like(acc)

    def gram(g, rows):
        block = jnp.concatenate(
            [pieces[g * UNROLL + u, t].reshape(side, cz) for u in range(UNROLL) for t in rows], axis=1)
        acc[...] += dot(block, block, ((1,), (1,)))

    acc_copy = pltpu.make_async_remote_copy(
        src_ref=acc, dst_ref=acc_far, send_sem=acc_send, recv_sem=acc_recv,
        device_id={"band": 1 - band}, device_id_type=MESH)

    edges = ((0, 0, can_recv[0]), (2, chunks - 1, can_recv[1]))

    def take_inner(o):
        hand_over(o, 1).wait_recv()
        for part, _, waits in edges:
            @pl.when(jnp.logical_not(waits))
            def _(part=part):
                hand_over(o, part).wait_recv()

        @pl.loop(first, last)
        def _(g):
            take_over(o, g)

    turned[...] = turn(yp, 0, pair(0, first, last))

    @pl.loop(0, count)
    def _(o):
        @pl.when(o + BEHIND < count)
        def _():
            start_faces(1, o + BEHIND, (0, 1))

        wait_faces(1, o, (2, 3, 4, 5))
        unpack_y(1, yp, o)
        correct_z(1, o)

        @pl.loop(0, (last - first + 1) // 2)
        def _(q):
            finish(o, pair(q, first, last), after(o, q, first, last))

        hand_over(o, 1).start()
        for part, _, waits in edges:
            @pl.when(jnp.logical_not(waits))
            def _(part=part):
                hand_over(o, part).start()

        @pl.when(o > 0)
        def _():
            take_inner(o - 1)

    take_inner(count - 1)

    half = tiles // 2

    @pl.loop(first, last)
    def _(g):
        gram(g, [band * half + t for t in range(half)])

    acc_copy.start()

    for part, g, waits in edges:
        @pl.when(waits)
        def _(part=part, g=g):
            turned[0:UNROLL * cy] = turn(yp, 0, (g,))

            @pl.loop(0, count)
            def _(o):
                wait_faces(1, o, (part // 2,))
                finish(o, (g,), (jnp.minimum(o + 1, count - 1), (g,)))
                hand_over(o, part).start()

    for part, g, waits in edges:
        @pl.when(waits)
        def _(part=part, g=g):
            @pl.loop(0, count)
            def _(o):
                hand_over(o, part).wait_recv()

            for o in range(count):
                take_over(o, g)

    acc_copy.wait()
    acc[...] += acc_far[...]

    for part, g, waits in edges:
        @pl.when(waits)
        def _(g=g):
            gram(g, range(tiles))

    same_row = (iota((side, side), 0) % 8) == (iota((side, side), 1) % 8)
    by_orbital = jnp.where(same_row, acc[...], 0.0).reshape(orbs, 16, side).sum(axis=1)
    column = iota((side, cz), 0) // 16
    first_part = by_orbital.astype(BF16).astype(F32)
    second_part = (by_orbital - first_part).astype(BF16).astype(F32)
    thirds = jnp.concatenate([first_part, second_part, by_orbital - first_part - second_part], axis=0).astype(BF16)
    gathered = dot(thirds, (iota((side, cz), 1) == column).astype(BF16))
    gathered = gathered[:orbs] + gathered[orbs:2 * orbs] + gathered[2 * orbs:]
    total = gathered[:count] + pltpu.roll(gathered[count:], orbs, 1)

    sums[grid_index] = total

    def reduce_copy(k):
        return pltpu.make_async_remote_copy(
            src_ref=sums.at[grid_index], dst_ref=sums.at[grid_index],
            send_sem=ar_send.at[k], recv_sem=ar_recv.at[k],
            device_id={"grid": grid_peer(k)}, device_id_type=MESH)

    @pl.loop(1, devices_grid)
    def _(k):
        reduce_copy(k).start()

    @pl.loop(0, count)
    def _(o):
        for stage in range(2):
            for d in range(6):
                @pl.when(can_send[d])
                def _(stage=stage, d=d):
                    face(stage, o, d).wait_send()
        for part in range(3):
            hand_over(o, part).wait_send()

    @pl.loop(1, devices_grid)
    def _(k):
        reduce_copy(k).wait_recv()

    total = sums[0]
    for k in range(1, devices_grid):
        total = total + sums[k]

    total = jnp.concatenate([total, pltpu.roll(total, cz - orbs, 1)], axis=0)
    row_id, lane_id = iota((orbs, cz), 0), iota((orbs, cz), 1)
    work = jnp.where(lane_id < orbs, total * (1.0 / volume), (lane_id == row_id + orbs).astype(F32))
    for k in range(orbs):
        ratio = jnp.where(row_id > k, work[:, k:k + 1] / work[k:k + 1, k:k + 1], 0.0)
        work = work - ratio * work[k:k + 1, :]
    pivots = jnp.sum(jnp.where(lane_id == row_id, work, 0.0), axis=1, keepdims=True)
    work = work / jnp.sqrt(pivots)

    out_rows = 8 * count
    work_high = work.astype(BF16).astype(F32)
    work_parts = jnp.concatenate([work_high, work - work_high], axis=0).astype(BF16)
    pick = iota((2 * out_rows, 2 * orbs), 0)
    pick = pick // out_rows * orbs + pick % out_rows // 8 + band * count
    rows_pick = (iota((2 * out_rows, 2 * orbs), 1) == pick).astype(BF16)
    lane = iota((cz, side), 1) // 16 + orbs
    lanes_pick = (iota((cz, side), 0) == lane).astype(BF16)
    full = dot(dot(rows_pick, work_parts).astype(BF16), lanes_pick)
    row, column = iota(full.shape, 0), iota(full.shape, 1)
    keep = (row % 8 == column % 8) & ((row < out_rows) | (column % 16 < 8))
    mix[...] = jnp.where(keep, full, 0.0).astype(BF16)

    @pl.loop(1, devices_grid)
    def _(k):
        reduce_copy(k).wait_send()


def rotate(pieces, mix, out_hbm, outv, out_sem):
    cx, tiles, _, count, _, cz = pieces.shape
    rows = 8 * count

    def store(x0):
        return pltpu.make_async_copy(
            outv.at[:, pl.ds(x0, UNROLL)], out_hbm.at[0, :, pl.ds(x0, UNROLL)], out_sem.at[x0 // UNROLL])

    for g in range(cx // UNROLL):
        x0 = g * UNROLL
        for u in range(UNROLL):
            for t in range(0, tiles, 2):
                pair = jnp.concatenate(
                    [pieces[x0 + u, t + k].reshape(4 * rows, cz) for k in range(2)], axis=1)
                both = dot(mix[...], pair)
                result = both[:rows] + both[rows:]
                for k in range(2):
                    outv[:, x0 + u, 8 * (t + k):8 * (t + k) + 8, :] = (
                        result[:, k * cz:(k + 1) * cz].reshape(count, 8, cz))
        store(x0).start()

    @pl.loop(0, cx // UNROLL)
    def _(g):
        store(g * UNROLL).wait()


def on_device(orbitals, potential):
    _, count, cx, cy, cz = orbitals.shape
    devices_grid = lax.axis_size("grid")
    parts = layout(devices_grid)
    volume = cx * cy * cz * devices_grid
    orbs = 2 * count
    side = 16 * orbs
    chunks = cx // UNROLL
    padded = (count, cx + 2 * REACH, cy + 2 * LEAD, cz)
    block = (count, cx, cy, cz)
    dma = pltpu.SemaphoreType.DMA
    any_spec = pl.BlockSpec(memory_space=pl.ANY)
    hbm_spec = pl.BlockSpec(memory_space=pltpu.HBM)
    vmem_spec = pl.BlockSpec(memory_space=pltpu.VMEM)
    pieces, mix = pl.pallas_call(
        functools.partial(kernel, parts, volume),
        out_shape=(pltpu.VMEM((cx, cy // 8, 2, count, 16, cz), BF16), pltpu.VMEM((16 * count, side), BF16)),
        in_specs=[hbm_spec, hbm_spec],
        out_specs=(vmem_spec, vmem_spec),
        scratch_shapes=[
            pltpu.VMEM(padded, F32), pltpu.VMEM(padded, F32),
            pltpu.VMEM(block, F32), pltpu.VMEM(block, F32), pltpu.VMEM((cx, cy, cz), F32),
            pltpu.VMEM((2, count, 2, REACH * cx, cz), F32), pltpu.VMEM((2, count, 2, REACH * cx, cz), F32),
            pltpu.VMEM((2, count, chunks, 8, cz), F32), pltpu.VMEM((2, count, 2, chunks, 8, cz), F32),
            pltpu.VMEM((count, chunks, 8, cz), F32),
            pltpu.VMEM((side, side), F32), pltpu.VMEM((side, side), F32),
            pltpu.VMEM((devices_grid, count, cz), F32), pltpu.VMEM((2 * cz, cz), BF16),
            pltpu.VMEM((2 * UNROLL * cy, cz), F32),
            dma((count + 1,)), dma((2, count, 6)), dma((2, count, 6)), dma((count, 3)), dma((count, 3)),
            dma, dma, dma((devices_grid,)), dma((devices_grid,)),
        ],
        compiler_params=pltpu.CompilerParams(
            collective_id=0, has_side_effects=True, vmem_limit_bytes=55 * 1024 * 1024),
    )(orbitals, potential)
    return pl.pallas_call(
        rotate,
        out_shape=jax.ShapeDtypeStruct(orbitals.shape, F32),
        in_specs=[vmem_spec, vmem_spec],
        out_specs=any_spec,
        scratch_shapes=[pltpu.VMEM(block, F32), dma((cx // UNROLL,))],
        compiler_params=pltpu.CompilerParams(vmem_limit_bytes=16 * 1024 * 1024),
    )(pieces, mix)


def solution(mesh):
    in_specs = (P("grid", "band", None, None, None), P("grid", None, None, None))
    out_specs = P("grid", "band", None, None, None)
    return jax.shard_map(
        on_device, mesh=mesh, in_specs=in_specs, out_specs=out_specs, check_vma=False
    )
```

```python
import functools

import jax
import jax.numpy as jnp
from jax import lax
from jax.experimental import pallas as pl
from jax.experimental.pallas import tpu as pltpu
from jax.sharding import PartitionSpec as P

COEFFS = (-49.0 / 18.0, 1.5, -0.15, 1.0 / 90.0)
CENTER = 5.75
HALF_WIDTH = 4.75
WHOLE = (270.0, -27.0, 2.0)
SCALE = -0.5 / (180.0 * HALF_WIDTH)
DIAGONAL = 3.0 * -0.5 * COEFFS[0] - CENTER
AHEAD = 6
BEHIND = 2
REACH = 3
LEAD = 8
UNROLL = 4
SLOT = 8
F32, BF16 = jnp.float32, jnp.bfloat16
MESH = pl.DeviceIdType.MESH


def layout(devices_grid):
    parts_x = max(2, devices_grid // 32)
    return (parts_x, parts_x, devices_grid // (parts_x * parts_x))


def dot(a, b, contract=((1,), (0,)), precision=None):
    return lax.dot_general(a, b, (contract, ((), ())), precision=precision, preferred_element_type=F32)


def halves(value):
    rounded = value.astype(BF16).astype(F32)
    return jnp.concatenate([rounded, value - rounded], axis=0).astype(BF16)


def iota(shape, dim):
    return lax.broadcasted_iota(jnp.int32, shape, dim)


def kernel(parts, volume, x_hbm, v_hbm, pieces, mix, xp, yp, y2, rem, pot, ypack, yrecv, zpack, zrecv, zcorr,
           acc, acc_far, sums, band_z, turned,
           load_sem, send_sem, recv_sem, y2_send, y2_recv, acc_send, acc_recv, ar_send, ar_recv):
    count, cx, cy, cz = y2.shape
    nx, ny, nz = parts
    sizes = (nx, ny, nz)
    devices_grid = nx * ny * nz
    strides = (ny * nz, nz, 1)
    grid_index = lax.axis_index("grid")
    band = lax.axis_index("band")
    pos = (grid_index // (ny * nz), grid_index // nz % ny, grid_index % nz)
    tiles = cy // 8
    orbs = 2 * count
    chunks = cx // UNROLL

    def loads(o):
        return pltpu.make_async_copy(
            x_hbm.at[0, o], xp.at[o, REACH:REACH + cx, LEAD:LEAD + cy], load_sem.at[o])

    pot_load = pltpu.make_async_copy(v_hbm.at[0], pot, load_sem.at[count])
    pot_load.start()

    @pl.loop(0, count)
    def _(o):
        loads(o).start()

    barrier = pltpu.get_barrier_semaphore()

    def grid_peer(k):
        return lax.rem(grid_index + k, devices_grid)

    @pl.loop(1, devices_grid)
    def _(k):
        pl.semaphore_signal(barrier, inc=1, device_id={"grid": grid_peer(k)}, device_id_type=MESH)

    pl.semaphore_signal(barrier, inc=1, device_id={"band": 1 - band}, device_id_type=MESH)
    pl.semaphore_wait(barrier, devices_grid)

    can_send = []
    for dim in range(3):
        can_send += [pos[dim] < sizes[dim] - 1, pos[dim] > 0]
    can_recv = [can_send[1], can_send[0], can_send[3], can_send[2], can_send[5], can_send[4]]

    def face(stage, o, d):
        field = (xp, yp)[stage]
        if d == 0:
            src, dst = field.at[o, cx:cx + REACH, LEAD:LEAD + cy], field.at[o, 0:REACH, LEAD:LEAD + cy]
        elif d == 1:
            src = field.at[o, REACH:2 * REACH, LEAD:LEAD + cy]
            dst = field.at[o, cx + REACH:cx + 2 * REACH, LEAD:LEAD + cy]
        elif d < 4:
            src, dst = ypack.at[stage, o, d - 2], yrecv.at[stage, o, d - 2]
        else:
            src, dst = zpack.at[stage, o], zrecv.at[stage, o, d - 4]
        if stage == 0 and d < 2:
            src = x_hbm.at[0, o, cx - REACH:cx] if d == 0 else x_hbm.at[0, o, 0:REACH]
        step = strides[d // 2] * (1 - 2 * (d % 2))
        return pltpu.make_async_remote_copy(
            src_ref=src, dst_ref=dst, send_sem=send_sem.at[stage, o, d], recv_sem=recv_sem.at[stage, o, d],
            device_id={"grid": grid_index + step}, device_id_type=MESH)

    def pack_y(stage, field, o):
        for x in range(cx):
            ypack[stage, o, 0, REACH * x:REACH * (x + 1), :] = field[o, REACH + x, LEAD + cy - REACH:LEAD + cy, :]
            ypack[stage, o, 1, REACH * x:REACH * (x + 1), :] = field[o, REACH + x, LEAD:LEAD + REACH, :]

    def unpack_y(stage, field, o):
        for x in range(cx):
            field[o, REACH + x, LEAD - REACH:LEAD, :] = yrecv[stage, o, 0, REACH * x:REACH * (x + 1), :]
            field[o, REACH + x, LEAD + cy:LEAD + cy + REACH, :] = yrecv[stage, o, 1, REACH * x:REACH * (x + 1), :]

    lane = iota((8, cz), 1)
    lane_slot = lane // SLOT

    def pack_z(stage, o, g, values):
        packed = pltpu.roll(values[0], REACH, 1)
        for slot in range(1, len(values)):
            packed = jnp.where(lane_slot == slot, pltpu.roll(values[slot], slot * SLOT + REACH, 1), packed)
        zpack[stage, o, g] = packed

    def correct_z(stage, o):
        own = zpack[stage, o]
        lanes = iota(own.shape, 2) % SLOT
        from_left = jnp.where(lanes < REACH, zrecv[stage, o, 0] - own, 0.0).reshape(-1, cz)
        right = (lanes >= REACH) & (lanes < 2 * REACH)
        from_right = jnp.where(right, zrecv[stage, o, 1] - own, 0.0).reshape(-1, cz)
        low_side, high_side = 0.0, 0.0
        for r in range(1, REACH + 1):
            low_side = low_side + WHOLE[r - 1] * pltpu.roll(from_left, r, 1)
            high_side = high_side + WHOLE[r - 1] * pltpu.roll(from_right, cz - r, 1)
        low_side, high_side = low_side.reshape(own.shape), high_side.reshape(own.shape)
        zcorr[o] = jnp.where(lanes < REACH, high_side, jnp.where(right, low_side, 0.0))

    edge = (lane < REACH) | (lane >= cz - REACH)

    def turn(field, some):
        start = jnp.concatenate(
            [field[o, pl.ds(g * UNROLL + REACH, UNROLL), LEAD:LEAD + cy, :].reshape(UNROLL * cy, cz) for o, g in some])
        high = start.astype(BF16)
        low = (start - high.astype(F32)).astype(BF16)
        return dot(jnp.concatenate([high, low], axis=1), band_z[...])

    def stencil(field, some, following, emit):
        coming = turn(field, following)
        for place, (o, g) in enumerate(some):
            x0 = g * UNROLL
            corr = zcorr[o, g]
            for t in range(tiles):
                rows = slice(LEAD + 8 * t, LEAD + 8 * t + 8)
                window = [field[o, x0 + i, rows, :] for i in range(UNROLL + 2 * REACH)]
                for u in range(UNROLL):
                    row = (place * UNROLL + u) * cy + 8 * t
                    total = pot[x0 + u, 8 * t:8 * t + 8, :] * window[u + REACH] + turned[row:row + 8]
                    for r in range(1, REACH + 1):
                        along_x = window[u + REACH + r] + window[u + REACH - r]
                        along_y = (field[o, x0 + u + REACH, rows.start + r:rows.stop + r, :]
                                   + field[o, x0 + u + REACH, rows.start - r:rows.stop - r, :])
                        total = total + WHOLE[r - 1] * (along_x + along_y)
                    fix = pltpu.roll(corr, (2 * cz - (t * UNROLL + u) * SLOT - REACH) % cz, 1)
                    emit(o, x0 + u, t, total + jnp.where(edge, fix, 0.0))
        turned[0:coming.shape[0]] = coming

    def wait_faces(stage, o, sides=tuple(range(6))):
        for d in sides:
            @pl.when(can_recv[d])
            def _(d=d):
                face(stage, o, d).wait_recv()

    def start_faces(stage, o, sides=tuple(range(6))):
        for d in sides:
            @pl.when(can_send[d])
            def _(d=d):
                face(stage, o, d).start()

    for o in range(AHEAD):
        start_faces(0, o, (0, 1))

    for d in range(6):
        @pl.when(jnp.logical_not(can_recv[d]))
        def _(d=d):
            @pl.loop(0, 2 * count)
            def _(i):
                stage, o = i // count, i % count
                if d < 2:
                    start = (0, cx + REACH)[d]
                    for k in range(REACH):
                        zero = jnp.zeros((cy, cz), F32)

                        @pl.when(stage == 0)
                        def _():
                            xp[o, start + k, LEAD:LEAD + cy, :] = zero

                        @pl.when(stage == 1)
                        def _():
                            yp[o, start + k, LEAD:LEAD + cy, :] = zero
                elif d < 4:
                    yrecv[stage, o, d - 2] = jnp.zeros(yrecv.shape[3:], F32)
                else:
                    zrecv[stage, o, d - 4] = jnp.zeros(zrecv.shape[3:], F32)

    def send_start(o):
        pack_y(0, xp, o)
        start_faces(0, o, (2, 3))

        @pl.loop(0, chunks // 4)
        def _(q):
            for k in range(4):
                g = 4 * q + k
                pack_z(0, o, g, [xp[o, g * UNROLL + u + REACH, LEAD + 8 * t:LEAD + 8 * t + 8, :]
                                 for t in range(tiles) for u in range(UNROLL)])

        start_faces(0, o, (4, 5))

    @pl.loop(0, count)
    def _(o):
        loads(o).wait()

        @pl.when(o < AHEAD)
        def _():
            send_start(o)

    apart = jnp.abs(iota((2 * cz, cz), 0) % cz - iota((2 * cz, cz), 1))
    weights = jnp.zeros((2 * cz, cz), F32)
    for r in range(1, REACH + 1):
        weights = jnp.where((apart == r) | (apart == cz - r), WHOLE[r - 1], weights)
    band_z[...] = weights.astype(BF16)
    pot_load.wait()

    @pl.loop(0, cx)
    def _(x):
        pot[x] = (pot[x] + DIAGONAL) * (1.0 / HALF_WIDTH / SCALE)

    def pair(o, q, low, high):
        return (o, low + 2 * q), (o, jnp.minimum(low + 2 * q + 1, high - 1))

    def after(o, q, low, high):
        more = 2 * q + 2 < high - low
        return pair(jnp.where(more, o, jnp.minimum(o + 1, count - 1)), jnp.where(more, q + 1, 0), low, high)

    turned[...] = turn(xp, ((0, 0), (0, 1)))

    @pl.loop(0, count)
    def _(o):
        wait_faces(0, o)

        @pl.when(o + AHEAD < count)
        def _():
            start_faces(0, o + AHEAD, (0, 1))
            send_start(o + AHEAD)

        unpack_y(0, xp, o)
        correct_z(0, o)

        @pl.loop(0, chunks // 2)
        def _(q):
            values = []

            def emit(o, x, t, value):
                yp[o, x + REACH, LEAD + 8 * t:LEAD + 8 * t + 8, :] = value
                values.append(value)

            stencil(xp, pair(o, q, 0, chunks), after(o, q, 0, chunks), emit)
            for k in range(2):
                pack_z(1, o, 2 * q + k, values[k * UNROLL * tiles:(k + 1) * UNROLL * tiles])

        start_faces(1, o, (4, 5))
        pack_y(1, yp, o)
        start_faces(1, o, (2, 3))

        @pl.when(o >= count - BEHIND)
        def _():
            start_faces(1, o - (count - BEHIND), (0, 1))

    first = jnp.where(can_recv[0], 1, 0)
    last = jnp.where(can_recv[1], chunks - 1, chunks)
    spans = ((0, UNROLL), (UNROLL, cx - 2 * UNROLL), (cx - UNROLL, UNROLL))

    def hand_over(o, part):
        planes = pl.ds(*spans[part])
        return pltpu.make_async_remote_copy(
            src_ref=y2.at[o, planes], dst_ref=rem.at[o, planes], send_sem=y2_send.at[o, part],
            recv_sem=y2_recv.at[o, part], device_id={"band": 1 - band}, device_id_type=MESH)

    def finish(some, following):
        def emit(o, x, t, value):
            start = xp[o, x + REACH, LEAD + 8 * t:LEAD + 8 * t + 8, :]
            value = value - start * (0.5 / SCALE / SCALE)
            y2[o, x, 8 * t:8 * t + 8, :] = value
            pieces[x, t, band, o] = halves(value)

        stencil(yp, some, following, emit)

    def take_over(o, g):
        for u in range(UNROLL):
            for t in range(tiles):
                pieces[g * UNROLL + u, t, 1 - band, o] = halves(rem[o, g * UNROLL + u, 8 * t:8 * t + 8, :])

    side = 16 * orbs
    acc[...] = jnp.zeros_like(acc)

    def gram(g, rows):
        block = jnp.concatenate(
            [pieces[g * UNROLL + u, t].reshape(side, cz) for u in range(UNROLL) for t in rows], axis=1)
        acc[...] += dot(block, block, ((1,), (1,)))

    acc_copy = pltpu.make_async_remote_copy(
        src_ref=acc, dst_ref=acc_far, send_sem=acc_send, recv_sem=acc_recv,
        device_id={"band": 1 - band}, device_id_type=MESH)

    edges = ((0, 0, can_recv[0]), (2, chunks - 1, can_recv[1]))

    def take_inner(o):
        hand_over(o, 1).wait_recv()
        for part, _, waits in edges:
            @pl.when(jnp.logical_not(waits))
            def _(part=part):
                hand_over(o, part).wait_recv()

        @pl.loop(first, last)
        def _(g):
            take_over(o, g)

    turned[...] = turn(yp, pair(0, 0, first, last))

    @pl.loop(0, count)
    def _(o):
        @pl.when(o % 4 < 3)
        def _():
            start_faces(1, o - o // 4 + BEHIND, (0, 1))

        wait_faces(1, o, (2, 3, 4, 5))
        unpack_y(1, yp, o)
        correct_z(1, o)

        @pl.loop(0, (last - first + 1) // 2)
        def _(q):
            finish(pair(o, q, first, last), after(o, q, first, last))

        hand_over(o, 1).start()
        for part, _, waits in edges:
            @pl.when(jnp.logical_not(waits))
            def _(part=part):
                hand_over(o, part).start()

        @pl.when(o > 0)
        def _():
            take_inner(o - 1)

    take_inner(count - 1)

    half = tiles // 2

    @pl.loop(first, last)
    def _(g):
        gram(g, [band * half + t for t in range(half)])

    acc_copy.start()

    for part, g, waits in edges:
        @pl.when(waits)
        def _(part=part, g=g):
            turned[...] = turn(yp, ((0, g), (1, g)))

            @pl.loop(0, count // 2)
            def _(h):
                o, following = 2 * h, jnp.minimum(2 * h + 2, count - 2)
                wait_faces(1, o, (part // 2,))
                wait_faces(1, o + 1, (part // 2,))
                finish(((o, g), (o + 1, g)), ((following, g), (following + 1, g)))
                hand_over(o, part).start()
                hand_over(o + 1, part).start()

    acc_copy.wait()
    acc[...] += acc_far[...]

    for part, g, waits in edges:
        @pl.when(waits)
        def _(part=part, g=g):
            @pl.loop(0, count)
            def _(o):
                hand_over(o, part).wait_recv()

            for o in range(count):
                take_over(o, g)

    for part, g, waits in edges:
        @pl.when(waits)
        def _(g=g):
            gram(g, range(tiles))

    same_row = (iota((side, side), 0) % 8) == (iota((side, side), 1) % 8)
    by_orbital = jnp.where(same_row, acc[...], 0.0).reshape(orbs, 16, side).sum(axis=1)
    column = iota((side, cz), 0) // 16
    first_part = by_orbital.astype(BF16).astype(F32)
    second_part = (by_orbital - first_part).astype(BF16).astype(F32)
    thirds = jnp.concatenate([first_part, second_part, by_orbital - first_part - second_part], axis=0).astype(BF16)
    gathered = dot(thirds, (iota((side, cz), 1) == column).astype(BF16))
    gathered = gathered[:orbs] + gathered[orbs:2 * orbs] + gathered[2 * orbs:]
    total = gathered[:count] + pltpu.roll(gathered[count:], orbs, 1)

    sums[grid_index] = total

    def reduce_copy(k):
        return pltpu.make_async_remote_copy(
            src_ref=sums.at[grid_index], dst_ref=sums.at[grid_index],
            send_sem=ar_send.at[k], recv_sem=ar_recv.at[k],
            device_id={"grid": grid_peer(k)}, device_id_type=MESH)

    def each_peer(act):
        if devices_grid <= 16:
            for k in range(1, devices_grid):
                act(k)
        else:
            pl.loop(1, devices_grid)(act)

    each_peer(lambda k: reduce_copy(k).start())

    @pl.loop(0, count)
    def _(o):
        for stage in range(2):
            for d in range(6):
                @pl.when(can_send[d])
                def _(stage=stage, d=d):
                    face(stage, o, d).wait_send()
        for part in range(3):
            hand_over(o, part).wait_send()

    each_peer(lambda k: reduce_copy(k).wait_recv())

    total = sums[0]
    for k in range(1, devices_grid):
        total = total + sums[k]

    total = jnp.concatenate([total, pltpu.roll(total, cz - orbs, 1)], axis=0)
    row_id, lane_id = iota((orbs, cz), 0), iota((orbs, cz), 1)
    work = jnp.where(lane_id < orbs, total * (1.0 / volume), (lane_id == row_id + orbs).astype(F32))
    for k in range(orbs):
        column = jnp.where(row_id > k, work[:, k:k + 1], 0.0)
        work = work - column * (work[k:k + 1, :] / work[k:k + 1, k:k + 1])
    pivots = jnp.sum(jnp.where(lane_id == row_id, work, 0.0), axis=1, keepdims=True)
    work = work / jnp.sqrt(pivots)

    out_rows = 8 * count
    work_high = work.astype(BF16).astype(F32)
    work_parts = jnp.concatenate([work_high, work - work_high], axis=0).astype(BF16)
    pick = iota((2 * out_rows, 2 * orbs), 0)
    pick = pick // out_rows * orbs + pick % out_rows // 8 + band * count
    rows_pick = (iota((2 * out_rows, 2 * orbs), 1) == pick).astype(BF16)
    lane = iota((cz, side), 1) // 16 + orbs
    lanes_pick = (iota((cz, side), 0) == lane).astype(BF16)
    full = dot(dot(rows_pick, work_parts).astype(BF16), lanes_pick)
    row, column = iota(full.shape, 0), iota(full.shape, 1)
    keep = (row % 8 == column % 8) & ((row < out_rows) | (column % 16 < 8))
    mix[...] = jnp.where(keep, full, 0.0).astype(BF16)

    @pl.loop(1, devices_grid)
    def _(k):
        reduce_copy(k).wait_send()


def rotate(pieces, mix, out_hbm, outv, out_sem):
    cx, tiles, _, count, _, cz = pieces.shape
    rows = 8 * count

    def store(x0):
        return pltpu.make_async_copy(
            outv.at[:, pl.ds(x0, UNROLL)], out_hbm.at[0, :, pl.ds(x0, UNROLL)], out_sem.at[x0 // UNROLL])

    for g in range(cx // UNROLL):
        x0 = g * UNROLL
        for u in range(UNROLL):
            for t in range(0, tiles, 2):
                pair = jnp.concatenate(
                    [pieces[x0 + u, t + k].reshape(4 * rows, cz) for k in range(2)], axis=1)
                both = dot(mix[...], pair)
                result = both[:rows] + both[rows:]
                for k in range(2):
                    outv[:, x0 + u, 8 * (t + k):8 * (t + k) + 8, :] = (
                        result[:, k * cz:(k + 1) * cz].reshape(count, 8, cz))
        store(x0).start()

    @pl.loop(0, cx // UNROLL)
    def _(g):
        store(g * UNROLL).wait()


def on_device(orbitals, potential):
    _, count, cx, cy, cz = orbitals.shape
    devices_grid = lax.axis_size("grid")
    parts = layout(devices_grid)
    volume = cx * cy * cz * devices_grid
    orbs = 2 * count
    side = 16 * orbs
    chunks = cx // UNROLL
    padded = (count, cx + 2 * REACH, cy + 2 * LEAD, cz)
    block = (count, cx, cy, cz)
    dma = pltpu.SemaphoreType.DMA
    any_spec = pl.BlockSpec(memory_space=pl.ANY)
    hbm_spec = pl.BlockSpec(memory_space=pltpu.HBM)
    vmem_spec = pl.BlockSpec(memory_space=pltpu.VMEM)
    pieces, mix = pl.pallas_call(
        functools.partial(kernel, parts, volume),
        out_shape=(pltpu.VMEM((cx, cy // 8, 2, count, 16, cz), BF16), pltpu.VMEM((16 * count, side), BF16)),
        in_specs=[hbm_spec, hbm_spec],
        out_specs=(vmem_spec, vmem_spec),
        scratch_shapes=[
            pltpu.VMEM(padded, F32), pltpu.VMEM(padded, F32),
            pltpu.VMEM(block, F32), pltpu.VMEM(block, F32), pltpu.VMEM((cx, cy, cz), F32),
            pltpu.VMEM((2, count, 2, REACH * cx, cz), F32), pltpu.VMEM((2, count, 2, REACH * cx, cz), F32),
            pltpu.VMEM((2, count, chunks, 8, cz), F32), pltpu.VMEM((2, count, 2, chunks, 8, cz), F32),
            pltpu.VMEM((count, chunks, 8, cz), F32),
            pltpu.VMEM((side, side), F32), pltpu.VMEM((side, side), F32),
            pltpu.VMEM((devices_grid, count, cz), F32), pltpu.VMEM((2 * cz, cz), BF16),
            pltpu.VMEM((2 * UNROLL * cy, cz), F32),
            dma((count + 1,)), dma((2, count, 6)), dma((2, count, 6)), dma((count, 3)), dma((count, 3)),
            dma, dma, dma((devices_grid,)), dma((devices_grid,)),
        ],
        compiler_params=pltpu.CompilerParams(
            collective_id=0, has_side_effects=True, vmem_limit_bytes=55 * 1024 * 1024),
    )(orbitals, potential)
    return pl.pallas_call(
        rotate,
        out_shape=jax.ShapeDtypeStruct(orbitals.shape, F32),
        in_specs=[vmem_spec, vmem_spec],
        out_specs=any_spec,
        scratch_shapes=[pltpu.VMEM(block, F32), dma((cx // UNROLL,))],
        compiler_params=pltpu.CompilerParams(vmem_limit_bytes=16 * 1024 * 1024),
    )(pieces, mix)


def solution(mesh):
    in_specs = (P("grid", "band", None, None, None), P("grid", None, None, None))
    out_specs = P("grid", "band", None, None, None)
    return jax.shard_map(
        on_device, mesh=mesh, in_specs=in_specs, out_specs=out_specs, check_vma=False
    )
```

```python
import functools

import jax
import jax.numpy as jnp
from jax import lax
from jax.experimental import pallas as pl
from jax.experimental.pallas import tpu as pltpu
from jax.sharding import PartitionSpec as P

COEFFS = (-49.0 / 18.0, 1.5, -0.15, 1.0 / 90.0)
CENTER = 5.75
HALF_WIDTH = 4.75
WHOLE = (270.0, -27.0, 2.0)
SCALE = -0.5 / (180.0 * HALF_WIDTH)
DIAGONAL = 3.0 * -0.5 * COEFFS[0] - CENTER
AHEAD = 8
BEHIND = 2
REACH = 3
LEAD = 8
UNROLL = 4
SLOT = 8
F32, BF16 = jnp.float32, jnp.bfloat16
MESH = pl.DeviceIdType.MESH


def layout(devices_grid):
    parts_x = max(2, devices_grid // 32)
    return (parts_x, parts_x, devices_grid // (parts_x * parts_x))


def dot(a, b, contract=((1,), (0,)), precision=None):
    return lax.dot_general(a, b, (contract, ((), ())), precision=precision, preferred_element_type=F32)


def halves(value):
    rounded = value.astype(BF16).astype(F32)
    return jnp.concatenate([rounded, value - rounded], axis=0).astype(BF16)


def iota(shape, dim):
    return lax.broadcasted_iota(jnp.int32, shape, dim)


def kernel(parts, volume, x_hbm, v_hbm, pieces, mix, xp, yp, y2, rem, pot, ypack, yrecv, zpack, zrecv, zcorr,
           acc, acc_far, sums, band_z, turned,
           load_sem, send_sem, recv_sem, y2_send, y2_recv, acc_send, acc_recv, ar_send, ar_recv):
    count, cx, cy, cz = y2.shape
    nx, ny, nz = parts
    sizes = (nx, ny, nz)
    devices_grid = nx * ny * nz
    strides = (ny * nz, nz, 1)
    grid_index = lax.axis_index("grid")
    band = lax.axis_index("band")
    pos = (grid_index // (ny * nz), grid_index // nz % ny, grid_index % nz)
    tiles = cy // 8
    orbs = 2 * count
    chunks = cx // UNROLL

    def loads(o):
        return pltpu.make_async_copy(
            x_hbm.at[0, o], xp.at[o, REACH:REACH + cx, LEAD:LEAD + cy], load_sem.at[o])

    pot_load = pltpu.make_async_copy(v_hbm.at[0], pot, load_sem.at[count])
    pot_load.start()

    @pl.loop(0, count)
    def _(o):
        loads(o).start()

    barrier = pltpu.get_barrier_semaphore()

    def grid_peer(k):
        return lax.rem(grid_index + k, devices_grid)

    @pl.loop(1, devices_grid)
    def _(k):
        pl.semaphore_signal(barrier, inc=1, device_id={"grid": grid_peer(k)}, device_id_type=MESH)

    pl.semaphore_signal(barrier, inc=1, device_id={"band": 1 - band}, device_id_type=MESH)
    pl.semaphore_wait(barrier, devices_grid)

    can_send = []
    for dim in range(3):
        can_send += [pos[dim] < sizes[dim] - 1, pos[dim] > 0]
    can_recv = [can_send[1], can_send[0], can_send[3], can_send[2], can_send[5], can_send[4]]

    def face(stage, o, d):
        field = (xp, yp)[stage]
        if d == 0:
            src, dst = field.at[o, cx:cx + REACH, LEAD:LEAD + cy], field.at[o, 0:REACH, LEAD:LEAD + cy]
        elif d == 1:
            src = field.at[o, REACH:2 * REACH, LEAD:LEAD + cy]
            dst = field.at[o, cx + REACH:cx + 2 * REACH, LEAD:LEAD + cy]
        elif d < 4:
            src, dst = ypack.at[stage, o, d - 2], yrecv.at[stage, o, d - 2]
        else:
            src, dst = zpack.at[stage, o], zrecv.at[stage, o, d - 4]
        if stage == 0 and d < 2:
            src = x_hbm.at[0, o, cx - REACH:cx] if d == 0 else x_hbm.at[0, o, 0:REACH]
        step = strides[d // 2] * (1 - 2 * (d % 2))
        return pltpu.make_async_remote_copy(
            src_ref=src, dst_ref=dst, send_sem=send_sem.at[stage, o, d], recv_sem=recv_sem.at[stage, o, d],
            device_id={"grid": grid_index + step}, device_id_type=MESH)

    def pack_y(stage, field, o):
        for x in range(cx):
            ypack[stage, o, 0, REACH * x:REACH * (x + 1), :] = field[o, REACH + x, LEAD + cy - REACH:LEAD + cy, :]
            ypack[stage, o, 1, REACH * x:REACH * (x + 1), :] = field[o, REACH + x, LEAD:LEAD + REACH, :]

    def unpack_y(stage, field, o):
        for x in range(cx):
            field[o, REACH + x, LEAD - REACH:LEAD, :] = yrecv[stage, o, 0, REACH * x:REACH * (x + 1), :]
            field[o, REACH + x, LEAD + cy:LEAD + cy + REACH, :] = yrecv[stage, o, 1, REACH * x:REACH * (x + 1), :]

    lane = iota((8, cz), 1)
    lane_slot = lane // SLOT

    def pack_z(stage, o, g, values):
        packed = pltpu.roll(values[0], REACH, 1)
        for slot in range(1, len(values)):
            packed = jnp.where(lane_slot == slot, pltpu.roll(values[slot], slot * SLOT + REACH, 1), packed)
        zpack[stage, o, g] = packed

    def correct_z(stage, o):
        own = zpack[stage, o]
        lanes = iota(own.shape, 2) % SLOT
        from_left = jnp.where(lanes < REACH, zrecv[stage, o, 0] - own, 0.0).reshape(-1, cz)
        right = (lanes >= REACH) & (lanes < 2 * REACH)
        from_right = jnp.where(right, zrecv[stage, o, 1] - own, 0.0).reshape(-1, cz)
        low_side, high_side = 0.0, 0.0
        for r in range(1, REACH + 1):
            low_side = low_side + WHOLE[r - 1] * pltpu.roll(from_left, r, 1)
            high_side = high_side + WHOLE[r - 1] * pltpu.roll(from_right, cz - r, 1)
        low_side, high_side = low_side.reshape(own.shape), high_side.reshape(own.shape)
        zcorr[o] = jnp.where(lanes < REACH, high_side, jnp.where(right, low_side, 0.0))

    edge = (lane < REACH) | (lane >= cz - REACH)

    def turn(field, some):
        start = jnp.concatenate(
            [field[o, pl.ds(g * UNROLL + REACH, UNROLL), LEAD:LEAD + cy, :].reshape(UNROLL * cy, cz) for o, g in some])
        high = start.astype(BF16)
        low = (start - high.astype(F32)).astype(BF16)
        return dot(jnp.concatenate([high, low], axis=1), band_z[...])

    def stencil(field, some, following, emit):
        coming = turn(field, following)
        for place, (o, g) in enumerate(some):
            x0 = g * UNROLL
            corr = zcorr[o, g]
            for t in range(tiles):
                rows = slice(LEAD + 8 * t, LEAD + 8 * t + 8)
                window = [field[o, x0 + i, rows, :] for i in range(UNROLL + 2 * REACH)]
                for u in range(UNROLL):
                    row = (place * UNROLL + u) * cy + 8 * t
                    total = pot[x0 + u, 8 * t:8 * t + 8, :] * window[u + REACH] + turned[row:row + 8]
                    for r in range(1, REACH + 1):
                        along_x = window[u + REACH + r] + window[u + REACH - r]
                        along_y = (field[o, x0 + u + REACH, rows.start + r:rows.stop + r, :]
                                   + field[o, x0 + u + REACH, rows.start - r:rows.stop - r, :])
                        total = total + WHOLE[r - 1] * (along_x + along_y)
                    fix = pltpu.roll(corr, (2 * cz - (t * UNROLL + u) * SLOT - REACH) % cz, 1)
                    emit(o, x0 + u, t, total + jnp.where(edge, fix, 0.0))
        turned[0:coming.shape[0]] = coming

    def wait_faces(stage, o, sides=tuple(range(6))):
        for d in sides:
            @pl.when(can_recv[d])
            def _(d=d):
                face(stage, o, d).wait_recv()

    def start_faces(stage, o, sides=tuple(range(6))):
        for d in sides:
            @pl.when(can_send[d])
            def _(d=d):
                face(stage, o, d).start()

    for o in range(AHEAD):
        start_faces(0, o, (0, 1))

    for d in range(6):
        @pl.when(jnp.logical_not(can_recv[d]))
        def _(d=d):
            @pl.loop(0, 2 * count)
            def _(i):
                stage, o = i // count, i % count
                if d < 2:
                    start = (0, cx + REACH)[d]
                    for k in range(REACH):
                        zero = jnp.zeros((cy, cz), F32)

                        @pl.when(stage == 0)
                        def _():
                            xp[o, start + k, LEAD:LEAD + cy, :] = zero

                        @pl.when(stage == 1)
                        def _():
                            yp[o, start + k, LEAD:LEAD + cy, :] = zero
                elif d < 4:
                    yrecv[stage, o, d - 2] = jnp.zeros(yrecv.shape[3:], F32)
                else:
                    zrecv[stage, o, d - 4] = jnp.zeros(zrecv.shape[3:], F32)

    def send_start(o):
        pack_y(0, xp, o)
        start_faces(0, o, (2, 3))

        @pl.loop(0, chunks // 4)
        def _(q):
            for k in range(4):
                g = 4 * q + k
                pack_z(0, o, g, [xp[o, g * UNROLL + u + REACH, LEAD + 8 * t:LEAD + 8 * t + 8, :]
                                 for t in range(tiles) for u in range(UNROLL)])

        start_faces(0, o, (4, 5))

    @pl.loop(0, count)
    def _(o):
        loads(o).wait()

        @pl.when(o < AHEAD)
        def _():
            send_start(o)

    apart = jnp.abs(iota((2 * cz, cz), 0) % cz - iota((2 * cz, cz), 1))
    weights = jnp.zeros((2 * cz, cz), F32)
    for r in range(1, REACH + 1):
        weights = jnp.where((apart == r) | (apart == cz - r), WHOLE[r - 1], weights)
    band_z[...] = weights.astype(BF16)
    pot_load.wait()

    @pl.loop(0, cx)
    def _(x):
        pot[x] = (pot[x] + DIAGONAL) * (1.0 / HALF_WIDTH / SCALE)

    def pair(o, q, low, high):
        return (o, low + 2 * q), (o, jnp.minimum(low + 2 * q + 1, high - 1))

    def after(o, q, low, high):
        more = 2 * q + 2 < high - low
        return pair(jnp.where(more, o, jnp.minimum(o + 1, count - 1)), jnp.where(more, q + 1, 0), low, high)

    turned[...] = turn(xp, ((0, 0), (0, 1)))

    @pl.loop(0, count)
    def _(o):
        wait_faces(0, o)

        @pl.when(o + AHEAD < count)
        def _():
            start_faces(0, o + AHEAD, (0, 1))
            send_start(o + AHEAD)

        unpack_y(0, xp, o)
        correct_z(0, o)

        @pl.loop(0, chunks // 2)
        def _(q):
            values = []

            def emit(o, x, t, value):
                yp[o, x + REACH, LEAD + 8 * t:LEAD + 8 * t + 8, :] = value
                values.append(value)

            stencil(xp, pair(o, q, 0, chunks), after(o, q, 0, chunks), emit)
            for k in range(2):
                pack_z(1, o, 2 * q + k, values[k * UNROLL * tiles:(k + 1) * UNROLL * tiles])

        start_faces(1, o, (4, 5))
        pack_y(1, yp, o)
        start_faces(1, o, (2, 3))

        @pl.when(o >= count - BEHIND)
        def _():
            start_faces(1, o - (count - BEHIND), (0, 1))

    first = jnp.where(can_recv[0], 1, 0)
    last = jnp.where(can_recv[1], chunks - 1, chunks)
    spans = ((0, UNROLL), (UNROLL, cx - 2 * UNROLL), (cx - UNROLL, UNROLL))

    def hand_over(o, part):
        planes = pl.ds(*spans[part])
        return pltpu.make_async_remote_copy(
            src_ref=y2.at[o, planes], dst_ref=rem.at[o, planes], send_sem=y2_send.at[o, part],
            recv_sem=y2_recv.at[o, part], device_id={"band": 1 - band}, device_id_type=MESH)

    def finish(some, following):
        def emit(o, x, t, value):
            start = xp[o, x + REACH, LEAD + 8 * t:LEAD + 8 * t + 8, :]
            value = value - start * (0.5 / SCALE / SCALE)
            y2[o, x, 8 * t:8 * t + 8, :] = value
            pieces[x, t, band, o] = halves(value)

        stencil(yp, some, following, emit)

    def take_over(o, g):
        for u in range(UNROLL):
            for t in range(tiles):
                pieces[g * UNROLL + u, t, 1 - band, o] = halves(rem[o, g * UNROLL + u, 8 * t:8 * t + 8, :])

    side = 16 * orbs
    acc[...] = jnp.zeros_like(acc)

    def gram(g, rows):
        block = jnp.concatenate(
            [pieces[g * UNROLL + u, t].reshape(side, cz) for u in range(UNROLL) for t in rows], axis=1)
        acc[...] += dot(block, block, ((1,), (1,)))

    acc_copy = pltpu.make_async_remote_copy(
        src_ref=acc, dst_ref=acc_far, send_sem=acc_send, recv_sem=acc_recv,
        device_id={"band": 1 - band}, device_id_type=MESH)

    edges = ((0, 0, can_recv[0]), (2, chunks - 1, can_recv[1]))

    def take_inner(o):
        hand_over(o, 1).wait_recv()
        for part, _, waits in edges:
            @pl.when(jnp.logical_not(waits))
            def _(part=part):
                hand_over(o, part).wait_recv()

        @pl.loop(first, last)
        def _(g):
            take_over(o, g)

    turned[...] = turn(yp, pair(0, 0, first, last))

    @pl.loop(0, count)
    def _(o):
        @pl.when(o % 4 < 3)
        def _():
            start_faces(1, o - o // 4 + BEHIND, (0, 1))

        wait_faces(1, o, (2, 3, 4, 5))
        unpack_y(1, yp, o)
        correct_z(1, o)

        @pl.loop(0, (last - first + 1) // 2)
        def _(q):
            finish(pair(o, q, first, last), after(o, q, first, last))

        hand_over(o, 1).start()
        for part, _, waits in edges:
            @pl.when(jnp.logical_not(waits))
            def _(part=part):
                hand_over(o, part).start()

        @pl.when(o > 0)
        def _():
            take_inner(o - 1)

    take_inner(count - 1)

    half = tiles // 2

    @pl.loop(first, last)
    def _(g):
        gram(g, [band * half + t for t in range(half)])

    acc_copy.start()

    for part, g, waits in edges:
        @pl.when(waits)
        def _(part=part, g=g):
            turned[...] = turn(yp, ((0, g), (1, g)))

            @pl.loop(0, count // 2)
            def _(h):
                o, following = 2 * h, jnp.minimum(2 * h + 2, count - 2)
                wait_faces(1, o, (part // 2,))
                wait_faces(1, o + 1, (part // 2,))
                finish(((o, g), (o + 1, g)), ((following, g), (following + 1, g)))
                hand_over(o, part).start()
                hand_over(o + 1, part).start()

    acc_copy.wait()
    acc[...] += acc_far[...]

    for part, g, waits in edges:
        @pl.when(waits)
        def _(part=part, g=g):
            @pl.loop(0, count)
            def _(o):
                hand_over(o, part).wait_recv()

            for o in range(count):
                take_over(o, g)

    for part, g, waits in edges:
        @pl.when(waits)
        def _(g=g):
            gram(g, range(tiles))

    same_row = (iota((side, side), 0) % 8) == (iota((side, side), 1) % 8)
    by_orbital = jnp.where(same_row, acc[...], 0.0).reshape(orbs, 16, side).sum(axis=1)
    column = iota((side, cz), 0) // 16
    first_part = by_orbital.astype(BF16).astype(F32)
    second_part = (by_orbital - first_part).astype(BF16).astype(F32)
    thirds = jnp.concatenate([first_part, second_part, by_orbital - first_part - second_part], axis=0).astype(BF16)
    gathered = dot(thirds, (iota((side, cz), 1) == column).astype(BF16))
    gathered = gathered[:orbs] + gathered[orbs:2 * orbs] + gathered[2 * orbs:]
    total = gathered[:count] + pltpu.roll(gathered[count:], orbs, 1)

    sums[grid_index] = total

    def reduce_copy(k):
        return pltpu.make_async_remote_copy(
            src_ref=sums.at[grid_index], dst_ref=sums.at[grid_index],
            send_sem=ar_send.at[k], recv_sem=ar_recv.at[k],
            device_id={"grid": grid_peer(k)}, device_id_type=MESH)

    def each_peer(act):
        if devices_grid <= 16:
            for k in range(1, devices_grid):
                act(k)
        else:
            pl.loop(1, devices_grid)(act)

    each_peer(lambda k: reduce_copy(k).start())

    @pl.loop(0, count)
    def _(o):
        for stage in range(2):
            for d in range(6):
                @pl.when(can_send[d])
                def _(stage=stage, d=d):
                    face(stage, o, d).wait_send()
        for part in range(3):
            hand_over(o, part).wait_send()

    each_peer(lambda k: reduce_copy(k).wait_recv())

    total = sums[0]
    for k in range(1, devices_grid):
        total = total + sums[k]

    total = jnp.concatenate([total, pltpu.roll(total, cz - orbs, 1)], axis=0)
    row_id, lane_id = iota((orbs, cz), 0), iota((orbs, cz), 1)
    work = jnp.where(lane_id < orbs, total * (1.0 / volume), (lane_id == row_id + orbs).astype(F32))
    for k in range(0, orbs, 8):
        block = range(k, k + 8)
        columns = {i: jnp.broadcast_to(work[:, i:i + 1], work.shape) for i in block}
        reduced = work
        for i in block:
            row = reduced[i:i + 1] / columns[i][i:i + 1]
            below = jnp.where(row_id > i, columns[i], 0.0)
            reduced = reduced - below * row
            for j in range(i + 1, k + 8):
                columns[j] = columns[j] - below * (columns[i][j:j + 1] / columns[i][i:i + 1])
        work = reduced
    pivots = jnp.sum(jnp.where(lane_id == row_id, work, 0.0), axis=1, keepdims=True)
    work = work / jnp.sqrt(pivots)

    out_rows = 8 * count
    work_high = work.astype(BF16).astype(F32)
    work_parts = jnp.concatenate([work_high, work - work_high], axis=0).astype(BF16)
    pick = iota((2 * out_rows, 2 * orbs), 0)
    pick = pick // out_rows * orbs + pick % out_rows // 8 + band * count
    rows_pick = (iota((2 * out_rows, 2 * orbs), 1) == pick).astype(BF16)
    lane = iota((cz, side), 1) // 16 + orbs
    lanes_pick = (iota((cz, side), 0) == lane).astype(BF16)
    full = dot(dot(rows_pick, work_parts).astype(BF16), lanes_pick)
    row, column = iota(full.shape, 0), iota(full.shape, 1)
    keep = (row % 8 == column % 8) & ((row < out_rows) | (column % 16 < 8))
    mix[...] = jnp.where(keep, full, 0.0).astype(BF16)

    @pl.loop(1, devices_grid)
    def _(k):
        reduce_copy(k).wait_send()


def rotate(pieces, mix, out_hbm, outv, out_sem):
    cx, tiles, _, count, _, cz = pieces.shape
    rows = 8 * count

    def store(x0):
        return pltpu.make_async_copy(
            outv.at[:, pl.ds(x0, UNROLL)], out_hbm.at[0, :, pl.ds(x0, UNROLL)], out_sem.at[x0 // UNROLL])

    for g in range(cx // UNROLL):
        x0 = g * UNROLL
        for u in range(UNROLL):
            for t in range(0, tiles, 2):
                pair = jnp.concatenate(
                    [pieces[x0 + u, t + k].reshape(4 * rows, cz) for k in range(2)], axis=1)
                both = dot(mix[...], pair)
                result = both[:rows] + both[rows:]
                for k in range(2):
                    outv[:, x0 + u, 8 * (t + k):8 * (t + k) + 8, :] = (
                        result[:, k * cz:(k + 1) * cz].reshape(count, 8, cz))
        store(x0).start()

    @pl.loop(0, cx // UNROLL)
    def _(g):
        store(g * UNROLL).wait()


def on_device(orbitals, potential):
    _, count, cx, cy, cz = orbitals.shape
    devices_grid = lax.axis_size("grid")
    parts = layout(devices_grid)
    volume = cx * cy * cz * devices_grid
    orbs = 2 * count
    side = 16 * orbs
    chunks = cx // UNROLL
    padded = (count, cx + 2 * REACH, cy + 2 * LEAD, cz)
    block = (count, cx, cy, cz)
    dma = pltpu.SemaphoreType.DMA
    any_spec = pl.BlockSpec(memory_space=pl.ANY)
    hbm_spec = pl.BlockSpec(memory_space=pltpu.HBM)
    vmem_spec = pl.BlockSpec(memory_space=pltpu.VMEM)
    pieces, mix = pl.pallas_call(
        functools.partial(kernel, parts, volume),
        out_shape=(pltpu.VMEM((cx, cy // 8, 2, count, 16, cz), BF16), pltpu.VMEM((16 * count, side), BF16)),
        in_specs=[hbm_spec, hbm_spec],
        out_specs=(vmem_spec, vmem_spec),
        scratch_shapes=[
            pltpu.VMEM(padded, F32), pltpu.VMEM(padded, F32),
            pltpu.VMEM(block, F32), pltpu.VMEM(block, F32), pltpu.VMEM((cx, cy, cz), F32),
            pltpu.VMEM((2, count, 2, REACH * cx, cz), F32), pltpu.VMEM((2, count, 2, REACH * cx, cz), F32),
            pltpu.VMEM((2, count, chunks, 8, cz), F32), pltpu.VMEM((2, count, 2, chunks, 8, cz), F32),
            pltpu.VMEM((count, chunks, 8, cz), F32),
            pltpu.VMEM((side, side), F32), pltpu.VMEM((side, side), F32),
            pltpu.VMEM((devices_grid, count, cz), F32), pltpu.VMEM((2 * cz, cz), BF16),
            pltpu.VMEM((2 * UNROLL * cy, cz), F32),
            dma((count + 1,)), dma((2, count, 6)), dma((2, count, 6)), dma((count, 3)), dma((count, 3)),
            dma, dma, dma((devices_grid,)), dma((devices_grid,)),
        ],
        compiler_params=pltpu.CompilerParams(
            collective_id=0, has_side_effects=True, vmem_limit_bytes=55 * 1024 * 1024),
    )(orbitals, potential)
    return pl.pallas_call(
        rotate,
        out_shape=jax.ShapeDtypeStruct(orbitals.shape, F32),
        in_specs=[vmem_spec, vmem_spec],
        out_specs=any_spec,
        scratch_shapes=[pltpu.VMEM(block, F32), dma((cx // UNROLL,))],
        compiler_params=pltpu.CompilerParams(vmem_limit_bytes=16 * 1024 * 1024),
    )(pieces, mix)


def solution(mesh):
    in_specs = (P("grid", "band", None, None, None), P("grid", None, None, None))
    out_specs = P("grid", "band", None, None, None)
    return jax.shard_map(
        on_device, mesh=mesh, in_specs=in_specs, out_specs=out_specs, check_vma=False
    )
```
